128 devices in a mesh: tile: 16 (over y, z_lo, core), frame: 8 (over z_hi, x).
Axes of the slice: x: 4, y: 4, z: 4 (z_hi: 2, z_lo: 2; z = z_hi * 2 + z_lo), core: 2. Of those that a mesh axis runs over, the one named last changes fastest.
Arguments:
- object_slices: float32 [2, 2, 4096, 1024], P(None, None, 'tile', 'frame'), may hold values from -6 to 6
- probe_modes: float32 [2, 2, 256, 256], replicated, may hold values from -3 to 3
- prop_phase: float32 [256, 256], replicated, may hold values from -3.140625 to 3.140625
- background: float32 [256, 256], replicated, may hold values from 0.1 to 1
- positions: int32 [256, 2], P(('tile', 'frame')), may hold values from 0 to 768, as said below
- counts: int32 [256, 256, 256], P(('tile', 'frame')), may hold values from 0 to 8
Outputs:
- object_grad: float32 [2, 2, 4096, 1024], P(None, None, 'tile', 'frame')
- probe_grad: float32 [2, 2, 256, 256], replicated
The draws below stay inside these ranges and needn't reach their ends.
Inputs may be any that keep to these rules, and one draw needn't show every extreme that they name: `positions`: rows lie in 0 to 256, columns in 0 to 768.
All inputs are finite; a program needn't handle non-finite values.
Results may differ from the reference program's by a relative error of at most 0.0003.
Values sent between devices are 32-bit elements; how exact they have to be, the bound alone decides.
A program may use at most 128 MiB of HBM per device.

```python
import math
import jax
import jax.numpy as jnp
from jax import lax

FRAME = 256
MODES = 2
SLICES = 2
TILE_ROWS = 256
COLS = 1024
HALO = 128
F_DEV = 2
NROWS = 4096
FRAMES = 256
N_FRAME = 8


def draw_positions(key, part):
    first_key, second_key = jax.random.split(jax.random.fold_in(key, 17))
    rows_drawn = jax.random.randint(first_key, (FRAMES,), 0, TILE_ROWS + 2 * HALO - FRAME + 1)
    cols_drawn = jax.random.randint(second_key, (FRAMES,), 0, COLS - FRAME + 1)
    return jnp.stack([rows_drawn, cols_drawn], axis=1).astype(jnp.int32)


def set_ends(entries, rng, low, top_value):
    longest = entries.shape.index(max(entries.shape))
    spots = []
    for shift in (0, 1):
        where = [jax.random.randint(jax.random.fold_in(rng, axis), (), 0, length) for axis, length in enumerate(entries.shape)]
        where[longest] = (where[longest] + shift) % entries.shape[longest]
        spots.append(tuple(where))
    return entries.at[spots[0]].set(low).at[spots[1]].set(top_value)


def block_scale(rng, shape, cuts, low, top_value):
    def one(axis_at, shards_of):
        heights = jax.random.uniform(jax.random.fold_in(jax.random.fold_in(rng, 6), axis_at), (shards_of,), jnp.float32, low / len(cuts), top_value / len(cuts))
        return jnp.repeat(jnp.exp(heights), shape[axis_at] // shards_of).reshape((-1,) + (1,) * (len(shape) - axis_at - 1))

    loudness = one(*cuts[0])
    for cut in cuts[1:]:
        loudness = loudness * one(*cut)
    return loudness


def bell_draw(stream_key, shape, width, reach, cuts=(), kind=jnp.bfloat16):
    drawn = jax.random.normal(stream_key, shape, jnp.float32) * width
    if len(cuts) > 0:
        drawn = block_scale(stream_key, shape, cuts, -0.22, 0.18) * drawn
    return jnp.clip(drawn, min=-reach, max=reach).astype(kind)


def setup_inputs(seed: int = 0) -> dict:
    streams_of = jax.random.split(jax.random.key(seed), 7)
    object_slices = bell_draw(streams_of[0], (SLICES, 2, NROWS, COLS), 1.0, 6.0, ((2, 16), (3, 8)), jnp.float32)
    probe_modes = bell_draw(streams_of[1], (MODES, 2, FRAME, FRAME), 0.35, 3.0, (), jnp.float32)
    prop_phase = jnp.clip(jax.random.uniform(streams_of[2], (FRAME, FRAME), jnp.float32, -3.140625, 3.140625), -3.140625, 3.140625)
    background = jnp.clip(jnp.exp(jax.random.uniform(streams_of[3], (FRAME, FRAME), jnp.float32, math.log(0.1), math.log(1.0))), 0.1, 1.0)
    positions = draw_positions(jax.random.fold_in(streams_of[6], 71), 0)
    counts = set_ends(jax.random.randint(streams_of[5], (FRAMES, FRAME, FRAME), 0, 9), jax.random.fold_in(streams_of[5], 1), 0, 8).astype(jnp.int32)
    return dict(object_slices=object_slices, probe_modes=probe_modes, prop_phase=prop_phase, background=background, positions=positions, counts=counts)


def matmul_high(left, right):
    return jnp.matmul(left, right, precision=lax.Precision.HIGHEST)


def dft_tables(length):
    index = jnp.arange(length, dtype=jnp.int32)
    product = (index[:, None] * index[None, :]) % length
    angles = product.astype(jnp.float32) * (-2.0 * 3.141592653589793 / length)
    scale = length ** -0.5
    return jnp.cos(angles) * scale, jnp.sin(angles) * scale


def transform(wave_re, wave_im, table_re, table_im):
    left_re = matmul_high(table_re, wave_re) - matmul_high(table_im, wave_im)
    left_im = matmul_high(table_re, wave_im) + matmul_high(table_im, wave_re)
    out_re = matmul_high(left_re, table_re) - matmul_high(left_im, table_im)
    out_im = matmul_high(left_re, table_im) + matmul_high(left_im, table_re)
    return out_re, out_im


def propagate(wave_re, wave_im, kern_re, kern_im, table_re, table_im):
    spec_re, spec_im = transform(wave_re, wave_im, table_re, table_im)
    spec_re, spec_im = spec_re * kern_re - spec_im * kern_im, spec_re * kern_im + spec_im * kern_re
    return transform(spec_re, spec_im, table_re, -table_im)


def frame_gradients(windows, probe_modes, prop_phase, background, measured, tables):
    table_re, table_im = tables
    batch_size = windows.shape[0]
    slice_count = windows.shape[1]
    mode_count = probe_modes.shape[0]
    length = probe_modes.shape[-1]
    kern_re = jnp.cos(prop_phase)
    kern_im = jnp.sin(prop_phase)
    wave_re = jnp.broadcast_to(probe_modes[:, 0][None], (batch_size, mode_count, length, length))
    wave_im = jnp.broadcast_to(probe_modes[:, 1][None], (batch_size, mode_count, length, length))
    incoming = []
    for layer_index in range(slice_count):
        obj_re = windows[:, layer_index, 0][:, None]
        obj_im = windows[:, layer_index, 1][:, None]
        incoming.append((wave_re, wave_im))
        wave_re, wave_im = wave_re * obj_re - wave_im * obj_im, wave_re * obj_im + wave_im * obj_re
        if layer_index < slice_count - 1:
            wave_re, wave_im = propagate(wave_re, wave_im, kern_re, kern_im, table_re, table_im)
    far_re, far_im = transform(wave_re, wave_im, table_re, table_im)
    intensity = jnp.sum(far_re * far_re + far_im * far_im, axis=1) + background
    weight = (1.0 - measured / intensity)[:, None]
    back_re, back_im = transform(weight * far_re, weight * far_im, table_re, -table_im)
    slice_terms = [None] * slice_count
    for layer_index in reversed(range(slice_count)):
        before_re, before_im = incoming[layer_index]
        obj_re = windows[:, layer_index, 0][:, None]
        obj_im = windows[:, layer_index, 1][:, None]
        grad_re = jnp.sum(before_re * back_re + before_im * back_im, axis=1)
        grad_im = jnp.sum(before_re * back_im - before_im * back_re, axis=1)
        slice_terms[layer_index] = jnp.stack([grad_re, grad_im], axis=1)
        back_re, back_im = back_re * obj_re + back_im * obj_im, back_im * obj_re - back_re * obj_im
        if layer_index > 0:
            back_re, back_im = propagate(back_re, back_im, kern_re, -kern_im, table_re, table_im)
    probe_term = jnp.sum(jnp.stack([back_re, back_im], axis=2), axis=0)
    return jnp.stack(slice_terms, axis=1), probe_term


def reference(object_slices, probe_modes, prop_phase, background, positions, counts):
    rows_all = object_slices.shape[2]
    padded = jnp.concatenate([object_slices[:, :, rows_all - HALO:], object_slices, object_slices[:, :, :HALO]], axis=2)
    tables = dft_tables(FRAME)
    per_tile = N_FRAME * F_DEV

    def advance(running, frame_item):
        grad_acc, probe_acc = running
        frame_place, measured, number = frame_item
        tile_index = number // per_tile
        zero_index = jnp.zeros((), jnp.int32)
        start_index = (zero_index, zero_index, (tile_index * TILE_ROWS + frame_place[0]).astype(jnp.int32), frame_place[1].astype(jnp.int32))
        window = lax.dynamic_slice(padded, start_index, (SLICES, 2, FRAME, FRAME))
        slice_terms, probe_term = frame_gradients(window[None], probe_modes, prop_phase, background, measured.astype(jnp.float32)[None], tables)
        current = lax.dynamic_slice(grad_acc, start_index, (SLICES, 2, FRAME, FRAME))
        grad_acc = lax.dynamic_update_slice(grad_acc, current + slice_terms[0], start_index)
        return (grad_acc, probe_acc + probe_term), None

    initial = (jnp.zeros(padded.shape, jnp.float32), jnp.zeros(probe_modes.shape, jnp.float32))
    numbers = jnp.arange(positions.shape[0], dtype=jnp.int32)
    (grad_acc, probe_grad), unused = lax.scan(advance, initial, (positions, counts, numbers))
    object_grad = grad_acc[:, :, HALO:HALO + rows_all]
    object_grad = object_grad.at[:, :, rows_all - HALO:].add(grad_acc[:, :, :HALO])
    object_grad = object_grad.at[:, :, :HALO].add(grad_acc[:, :, HALO + rows_all:])
    return object_grad, probe_grad
```

```python
import functools
import numpy as np
import ml_dtypes
import jax
import jax.numpy as jnp
from jax import lax
from jax.experimental import pallas as pl
from jax.experimental.pallas import tpu as pltpu
from jax.sharding import PartitionSpec as P

FRAME = 256
HALF = 128
SLICES = 2
MODES = 2
HALO = 128
ROWS_EXT = 512
STRIPS = 8
WIN_ROWS = 264
WIN_COLS = 384
CHUNK = 32
F32 = jnp.float32
BF16 = jnp.bfloat16


def dft_constants():
    k = np.arange(HALF)[:, None]
    n = np.arange(HALF)[None, :]
    mats = []
    for odd in (0, 1):
        turns = ((2 * k + odd) * n) % FRAME
        angle = -2.0 * np.pi * turns / FRAME
        c, s = np.cos(angle) / 16.0, np.sin(angle) / 16.0
        mats.append(np.block([[c, -s], [s, c]]))
    even, odd = mats
    lefts, rights = [], []
    for m in (even, odd, even.T, odd.T):
        hi = m.astype(ml_dtypes.bfloat16)
        lo = (m - hi.astype(np.float64)).astype(ml_dtypes.bfloat16)
        lefts.append(np.concatenate([hi, hi, lo], axis=1))
        rights.append(np.concatenate([hi, hi, lo], axis=0))
    perm = np.zeros((FRAME, FRAME))
    order = np.concatenate([np.arange(0, FRAME, 2), np.arange(1, FRAME, 2)])
    perm[np.arange(FRAME), order] = 1.0
    perms = np.stack([perm, perm.T]).astype(ml_dtypes.bfloat16)
    return np.stack(lefts), np.stack(rights), perms


def mm(a, b):
    return jnp.dot(a, b, preferred_element_type=F32)


def parts3(x):
    a = x.astype(BF16)
    r = x - a.astype(F32)
    b = r.astype(BF16)
    c = (r - b.astype(F32)).astype(BF16)
    return a, b, c


def reorder_exact(x, perm, perm_t):
    a, b, c = parts3(x)
    y = mm(perm, a) + mm(perm, b) + mm(perm, c)
    a, b, c = parts3(y)
    return mm(a, perm_t) + mm(b, perm_t) + mm(c, perm_t)


def frame_kernel(
    pos_ref, ext_ref, probe_ref, phase_ref, back_ref, counts_ref, left_ref, right_ref, perm_ref,
    grad_ref, probe_out_ref,
    win, obj, kern, bg, cnt, wave, u1, rop, lop, tmp, freq, win_sems,
):
    def corner(f):
        r = pos_ref[f, 0]
        c = pos_ref[f, 1]
        r8 = jnp.minimum(r // 8, 31) * 8
        cs = jnp.minimum(c // HALF, 5)
        return r, c, pl.multiple_of(r8, 8), cs

    def window_copies(f):
        _, _, r8, cs = corner(f)
        return [
            pltpu.make_async_copy(
                ext_ref.at[cs + j, :, :, pl.ds(r8, WIN_ROWS), :],
                win.at[f, :, :, :, pl.ds(j * HALF, HALF)],
                win_sems.at[f, j],
            )
            for j in range(3)
        ]

    for f in range(2):
        for copy in window_copies(f):
            copy.start()

    perm, perm_t = perm_ref[0], perm_ref[1]
    bg[...] = reorder_exact(back_ref[...], perm, perm_t)
    phase = reorder_exact(phase_ref[...], perm, perm_t)
    kern[0] = jnp.cos(phase)
    kern[1] = jnp.sin(phase)
    for f in range(2):
        half = mm(perm, counts_ref[f].astype(F32).astype(BF16)).astype(BF16)
        cnt[f] = mm(half, perm_t)

    grad_ref[...] = jnp.zeros_like(grad_ref)

    def put_right(m, parity, rows, x):
        hi = x.astype(BF16)
        lo = (x - hi.astype(F32)).astype(BF16)
        rop[m, parity, rows, 0:256] = hi
        rop[m, parity, rows, 256:512] = lo
        rop[m, parity, rows, 512:768] = hi

    def put_left(m, parity, start, x):
        hi = x.astype(BF16)
        lo = (x - hi.astype(F32)).astype(BF16)
        n = x.shape[0]
        lop[m, parity, pl.ds(start, n), :] = hi
        lop[m, parity, pl.ds(256 + start, n), :] = lo
        lop[m, parity, pl.ds(512 + start, n), :] = hi

    def forward(m, produce):
        for q in range(FRAME // CHUNK):
            rows = pl.ds(q * CHUNK, CHUNK)
            re, im = produce(m, rows)
            a, b = re[:, :HALF], re[:, HALF:]
            c, d = im[:, :HALF], im[:, HALF:]
            put_right(m, 0, rows, jnp.concatenate([a + b, c + d], axis=1))
            put_right(m, 1, rows, jnp.concatenate([a - b, c - d], axis=1))
        tmp[m, 0] = mm(rop[m, 0], right_ref[2])
        tmp[m, 1] = mm(rop[m, 1], right_ref[3])
        for q in range(HALF // CHUNK):
            top = pl.ds(q * CHUNK, CHUNK)
            bot = pl.ds(HALF + q * CHUNK, CHUNK)
            et, eb = tmp[m, 0, top, :], tmp[m, 0, bot, :]
            ot, ob = tmp[m, 1, top, :], tmp[m, 1, bot, :]
            for parity, e, o in ((0, et + eb, ot + ob), (1, et - eb, ot - ob)):
                put_left(m, parity, q * CHUNK, jnp.concatenate([e[:, :HALF], o[:, :HALF]], axis=1))
                put_left(m, parity, HALF + q * CHUNK, jnp.concatenate([e[:, HALF:], o[:, HALF:]], axis=1))
        freq[m, 0] = mm(left_ref[0], lop[m, 0])
        freq[m, 1] = mm(left_ref[1], lop[m, 1])

    def backward(m, modify, consume):
        for parity in range(2):
            for q in range(HALF // CHUNK):
                top = pl.ds(q * CHUNK, CHUNK)
                bot = pl.ds(HALF + q * CHUNK, CHUNK)
                table_rows = pl.ds(parity * HALF + q * CHUNK, CHUNK)
                re, im = modify(table_rows, freq[m, parity, top, :], freq[m, parity, bot, :])
                put_left(m, parity, q * CHUNK, re)
                put_left(m, parity, HALF + q * CHUNK, im)
        tmp[m, 0] = mm(left_ref[2], lop[m, 0])
        tmp[m, 1] = mm(left_ref[3], lop[m, 1])
        for q in range(HALF // CHUNK):
            top = pl.ds(q * CHUNK, CHUNK)
            bot = pl.ds(HALF + q * CHUNK, CHUNK)
            gr, gi = tmp[m, 0, top, :], tmp[m, 0, bot, :]
            hr, hi = tmp[m, 1, top, :], tmp[m, 1, bot, :]
            for rows, re, im in ((top, gr + hr, gi + hi), (bot, gr - hr, gi - hi)):
                put_right(m, 0, rows, jnp.concatenate([re[:, :HALF], im[:, :HALF]], axis=1))
                put_right(m, 1, rows, jnp.concatenate([re[:, HALF:], im[:, HALF:]], axis=1))
        tmp[m, 0] = mm(rop[m, 0], right_ref[0])
        tmp[m, 1] = mm(rop[m, 1], right_ref[1])
        for q in range(FRAME // CHUNK):
            rows = pl.ds(q * CHUNK, CHUNK)
            g, h = tmp[m, 0, rows, :], tmp[m, 1, rows, :]
            re = jnp.concatenate([g[:, :HALF] + h[:, :HALF], g[:, :HALF] - h[:, :HALF]], axis=1)
            im = jnp.concatenate([g[:, HALF:] + h[:, HALF:], g[:, HALF:] - h[:, HALF:]], axis=1)
            consume(m, rows, re, im)

    @pl.loop(0, 2)
    def _(f):
        r, c, r8, cs = corner(f)
        row_shift = r - r8
        col_shift = c - cs * HALF
        for copy in window_copies(f):
            copy.wait()

        for s in range(SLICES):
            for p in range(2):
                for q in range(FRAME // CHUNK):
                    x = win[f, s, p, pl.ds(q * CHUNK, CHUNK + 8), :]
                    x = pltpu.roll(x, lax.rem(WIN_COLS - col_shift, WIN_COLS), 1)[:, :FRAME]
                    x = pltpu.roll(x, lax.rem(CHUNK + 8 - row_shift, CHUNK + 8), 0)
                    obj[s, p, pl.ds(q * CHUNK, CHUNK), :] = x[:CHUNK]

        def enter(m, rows):
            pr, pi = probe_ref[m, 0, rows, :], probe_ref[m, 1, rows, :]
            a, b = obj[0, 0, rows, :], obj[0, 1, rows, :]
            return pr * a - pi * b, pr * b + pi * a

        def through(m, rows):
            ur, ui = u1[m, 0, rows, :], u1[m, 1, rows, :]
            a, b = obj[1, 0, rows, :], obj[1, 1, rows, :]
            return ur * a - ui * b, ur * b + ui * a

        def returning(m, rows):
            hr, hi = wave[m, 0, rows, :], wave[m, 1, rows, :]
            a, b = obj[1, 0, rows, :], obj[1, 1, rows, :]
            return hr * a + hi * b, hi * a - hr * b

        def propagator(rows, re, im):
            kr, ki = kern[0, rows, :], kern[1, rows, :]
            return re * kr - im * ki, re * ki + im * kr

        def adjoint(rows, re, im):
            kr, ki = kern[0, rows, :], kern[1, rows, :]
            return re * kr + im * ki, im * kr - re * ki

        def weighted(rows, re, im):
            w = cnt[f, rows, :]
            return re * w, im * w

        def keep_u1(m, rows, re, im):
            u1[m, 0, rows, :] = re
            u1[m, 1, rows, :] = im

        def keep_wave(m, rows, re, im):
            wave[m, 0, rows, :] = re
            wave[m, 1, rows, :] = im

        def scatter(s, source):
            for q in range(FRAME // CHUNK):
                rows = pl.ds(q * CHUNK, CHUNK)
                target = pl.ds(pl.multiple_of(r8 + q * CHUNK, 8), CHUNK + 8)
                gr = gi = None
                for m in range(MODES):
                    ur, ui = source(m, rows)
                    hr, hi = wave[m, 0, rows, :], wave[m, 1, rows, :]
                    tr, ti = ur * hr + ui * hi, ur * hi - ui * hr
                    gr, gi = (tr, ti) if gr is None else (gr + tr, gi + ti)
                below = jnp.zeros((8, FRAME), F32)
                beside = jnp.zeros((CHUNK + 8, HALF), F32)
                for p, g in enumerate((gr, gi)):
                    tall = pltpu.roll(jnp.concatenate([g, below], axis=0), row_shift, 0)
                    wide = pltpu.roll(jnp.concatenate([tall, beside], axis=1), col_shift, 1)
                    for j in range(3):
                        grad_ref[cs + j, s, p, target, :] += wide[:, j * HALF:(j + 1) * HALF]

        for m in range(MODES):
            forward(m, enter)
        for m in range(MODES):
            backward(m, propagator, keep_u1)
        for m in range(MODES):
            forward(m, through)
        for parity in range(2):
            for q in range(HALF // CHUNK):
                top = pl.ds(q * CHUNK, CHUNK)
                bot = pl.ds(HALF + q * CHUNK, CHUNK)
                rows = pl.ds(parity * HALF + q * CHUNK, CHUNK)
                level = bg[rows, :]
                for m in range(MODES):
                    re, im = freq[m, parity, top, :], freq[m, parity, bot, :]
                    level = level + re * re + im * im
                cnt[f, rows, :] = 1.0 - cnt[f, rows, :] / level
        for m in range(MODES):
            backward(m, weighted, keep_wave)
        scatter(1, lambda m, rows: (u1[m, 0, rows, :], u1[m, 1, rows, :]))
        for m in range(MODES):
            forward(m, returning)
        for m in range(MODES):
            backward(m, adjoint, keep_wave)
        scatter(0, lambda m, rows: (probe_ref[m, 0, rows, :], probe_ref[m, 1, rows, :]))
        for m in range(MODES):
            for q in range(FRAME // CHUNK):
                rows = pl.ds(q * CHUNK, CHUNK)
                hr, hi = wave[m, 0, rows, :], wave[m, 1, rows, :]
                a, b = obj[0, 0, rows, :], obj[0, 1, rows, :]
                tr, ti = hr * a + hi * b, hi * a - hr * b

                @pl.when(f == 0)
                def _():
                    probe_out_ref[m, 0, rows, :] = tr
                    probe_out_ref[m, 1, rows, :] = ti

                @pl.when(f != 0)
                def _():
                    probe_out_ref[m, 0, rows, :] += tr
                    probe_out_ref[m, 1, rows, :] += ti


def frame_terms(positions, ext, probe_modes, prop_phase, background, counts):
    lefts, rights, perms = dft_constants()
    vmem = pl.BlockSpec(memory_space=pltpu.VMEM)
    square = (FRAME, FRAME)
    return pl.pallas_call(
        frame_kernel,
        out_shape=(
            jax.ShapeDtypeStruct((STRIPS, SLICES, 2, ROWS_EXT, HALF), F32),
            jax.ShapeDtypeStruct((MODES, 2) + square, F32),
        ),
        in_specs=[pl.BlockSpec(memory_space=pltpu.SMEM), pl.BlockSpec(memory_space=pl.ANY)] + [vmem] * 7,
        out_specs=(vmem, vmem),
        scratch_shapes=[
            pltpu.VMEM((2, SLICES, 2, WIN_ROWS, WIN_COLS), F32),
            pltpu.VMEM((SLICES, 2) + square, F32),
            pltpu.VMEM((2,) + square, F32),
            pltpu.VMEM(square, F32),
            pltpu.VMEM((2,) + square, F32),
            pltpu.VMEM((MODES, 2) + square, F32),
            pltpu.VMEM((MODES, 2) + square, F32),
            pltpu.VMEM((MODES, 2, FRAME, 3 * FRAME), BF16),
            pltpu.VMEM((MODES, 2, 3 * FRAME, FRAME), BF16),
            pltpu.VMEM((MODES, 2) + square, F32),
            pltpu.VMEM((MODES, 2) + square, F32),
            pltpu.SemaphoreType.DMA((2, 3)),
        ],
        compiler_params=pltpu.CompilerParams(vmem_limit_bytes=48 << 20),
        name="frame_terms",
    )(positions, ext, probe_modes, prop_phase, background, counts,
      jnp.asarray(lefts), jnp.asarray(rights), jnp.asarray(perms))


def shifted(array, axis, by):
    count = lax.axis_size(axis)
    return lax.ppermute(array, axis, [(i, (i + by) % count) for i in range(count)])


def shards(object_slices, probe_modes, prop_phase, background, positions, counts):
    rows_own = object_slices.shape[2]
    before = shifted(object_slices[:, :, rows_own - HALO:], "tile", 1)
    after = shifted(object_slices[:, :, :HALO], "tile", -1)
    strip = jnp.concatenate([before, object_slices, after], axis=2)
    ext = lax.all_gather(strip, "frame", axis=0, tiled=False)
    grads, probe_term = frame_terms(positions, ext, probe_modes, prop_phase, background, counts)
    probe_grad = lax.psum(probe_term, ("tile", "frame"))
    summed = lax.psum_scatter(grads, "frame", scatter_dimension=0, tiled=False)
    from_below = shifted(summed[:, :, :HALO], "tile", -1)
    from_above = shifted(summed[:, :, HALO + rows_own:], "tile", 1)
    object_grad = summed[:, :, HALO:HALO + rows_own]
    object_grad = object_grad.at[:, :, rows_own - HALO:].add(from_below)
    object_grad = object_grad.at[:, :, :HALO].add(from_above)
    return object_grad, probe_grad


def solution(mesh):
    in_specs = (
        P(None, None, "tile", "frame"),
        P(),
        P(),
        P(),
        P(("tile", "frame"), None),
        P(("tile", "frame"), None, None),
    )
    out_specs = (P(None, None, "tile", "frame"), P())
    return jax.shard_map(shards, mesh=mesh, in_specs=in_specs, out_specs=out_specs, check_vma=False)
```

```python
import numpy as np
import ml_dtypes
import jax
import jax.numpy as jnp
from jax import lax
from jax.experimental import pallas as pl
from jax.experimental.pallas import tpu as pltpu
from jax.sharding import PartitionSpec as P

FRAME = 256
HALF = 128
SLICES = 2
MODES = 2
HALO = 128
ROWS_EXT = 512
STRIPS = 8
WIN_ROWS = 264
WIN_COLS = 384
CHUNK = 32
F32 = jnp.float32
BF16 = jnp.bfloat16


def dft_constants():
    k = np.arange(HALF)[:, None]
    n = np.arange(HALF)[None, :]
    mats = []
    for odd in (0, 1):
        turns = ((2 * k + odd) * n) % FRAME
        angle = -2.0 * np.pi * turns / FRAME
        c, s = np.cos(angle) / 16.0, np.sin(angle) / 16.0
        mats.append(np.block([[c, -s], [s, c]]))
    even, odd = mats
    lefts, rights = [], []
    for m in (even, odd, even.T, odd.T):
        hi = m.astype(ml_dtypes.bfloat16)
        lo = (m - hi.astype(np.float64)).astype(ml_dtypes.bfloat16)
        lefts.append(np.concatenate([hi, hi, lo], axis=1))
        rights.append(np.concatenate([hi, hi, lo], axis=0))
    perm = np.zeros((FRAME, FRAME))
    order = np.concatenate([np.arange(0, FRAME, 2), np.arange(1, FRAME, 2)])
    perm[np.arange(FRAME), order] = 1.0
    perms = np.stack([perm, perm.T]).astype(ml_dtypes.bfloat16)
    return np.stack(lefts), np.stack(rights), perms


def mm(a, b):
    return jnp.dot(a, b, preferred_element_type=F32)


def parts3(x):
    a = x.astype(BF16)
    r = x - a.astype(F32)
    b = r.astype(BF16)
    c = (r - b.astype(F32)).astype(BF16)
    return a, b, c


def reorder_exact(x, perm, perm_t):
    a, b, c = parts3(x)
    y = mm(perm, a) + mm(perm, b) + mm(perm, c)
    a, b, c = parts3(y)
    return mm(a, perm_t) + mm(b, perm_t) + mm(c, perm_t)


def frame_kernel(
    pos_ref, ext_ref, probe_ref, phase_ref, back_ref, counts_ref, left_ref, right_ref, perm_ref,
    grad_ref, probe_out_ref,
    win, obj, kern, bg, cnt, wave, u1, rop, lop, tmp, freq, win_sems,
):
    def corner(f):
        r = pos_ref[f, 0]
        c = pos_ref[f, 1]
        r8 = jnp.minimum(r // 8, 31) * 8
        cs = jnp.minimum(c // HALF, 5)
        return r, c, pl.multiple_of(r8, 8), cs

    def window_copies(f):
        _, _, r8, cs = corner(f)
        return [
            pltpu.make_async_copy(
                ext_ref.at[cs + j, :, :, pl.ds(r8, WIN_ROWS), :],
                win.at[f, :, :, :, pl.ds(j * HALF, HALF)],
                win_sems.at[f, j],
            )
            for j in range(3)
        ]

    for f in range(2):
        for copy in window_copies(f):
            copy.start()

    perm, perm_t = perm_ref[0], perm_ref[1]
    bg[...] = reorder_exact(back_ref[...], perm, perm_t)
    phase = reorder_exact(phase_ref[...], perm, perm_t)
    kern[0] = jnp.cos(phase)
    kern[1] = jnp.sin(phase)
    for f in range(2):
        half = mm(perm, counts_ref[f].astype(F32).astype(BF16)).astype(BF16)
        cnt[f] = mm(half, perm_t)

    grad_ref[...] = jnp.zeros_like(grad_ref)

    def put_right(m, parity, rows, x):
        hi = x.astype(BF16)
        lo = (x - hi.astype(F32)).astype(BF16)
        rop[m, parity, rows, 0:256] = hi
        rop[m, parity, rows, 256:512] = lo
        rop[m, parity, rows, 512:768] = hi

    def put_left(m, parity, start, x):
        hi = x.astype(BF16)
        lo = (x - hi.astype(F32)).astype(BF16)
        n = x.shape[0]
        lop[m, parity, pl.ds(start, n), :] = hi
        lop[m, parity, pl.ds(256 + start, n), :] = lo
        lop[m, parity, pl.ds(512 + start, n), :] = hi

    def forward(m, produce):
        for q in range(FRAME // CHUNK):
            rows = pl.ds(q * CHUNK, CHUNK)
            re, im = produce(m, rows)
            a, b = re[:, :HALF], re[:, HALF:]
            c, d = im[:, :HALF], im[:, HALF:]
            put_right(m, 0, rows, jnp.concatenate([a + b, c + d], axis=1))
            put_right(m, 1, rows, jnp.concatenate([a - b, c - d], axis=1))
        tmp[m, 0] = mm(rop[m, 0], right_ref[2])
        tmp[m, 1] = mm(rop[m, 1], right_ref[3])
        for q in range(HALF // CHUNK):
            top = pl.ds(q * CHUNK, CHUNK)
            bot = pl.ds(HALF + q * CHUNK, CHUNK)
            et, eb = tmp[m, 0, top, :], tmp[m, 0, bot, :]
            ot, ob = tmp[m, 1, top, :], tmp[m, 1, bot, :]
            for parity, e, o in ((0, et + eb, ot + ob), (1, et - eb, ot - ob)):
                put_left(m, parity, q * CHUNK, jnp.concatenate([e[:, :HALF], o[:, :HALF]], axis=1))
                put_left(m, parity, HALF + q * CHUNK, jnp.concatenate([e[:, HALF:], o[:, HALF:]], axis=1))
        freq[m, 0] = mm(left_ref[0], lop[m, 0])
        freq[m, 1] = mm(left_ref[1], lop[m, 1])

    def backward(m, modify, consume):
        for parity in range(2):
            for q in range(HALF // CHUNK):
                top = pl.ds(q * CHUNK, CHUNK)
                bot = pl.ds(HALF + q * CHUNK, CHUNK)
                table_rows = pl.ds(parity * HALF + q * CHUNK, CHUNK)
                re, im = modify(table_rows, freq[m, parity, top, :], freq[m, parity, bot, :])
                put_left(m, parity, q * CHUNK, re)
                put_left(m, parity, HALF + q * CHUNK, im)
        tmp[m, 0] = mm(left_ref[2], lop[m, 0])
        tmp[m, 1] = mm(left_ref[3], lop[m, 1])
        for q in range(HALF // CHUNK):
            top = pl.ds(q * CHUNK, CHUNK)
            bot = pl.ds(HALF + q * CHUNK, CHUNK)
            gr, gi = tmp[m, 0, top, :], tmp[m, 0, bot, :]
            hr, hi = tmp[m, 1, top, :], tmp[m, 1, bot, :]
            for rows, re, im in ((top, gr + hr, gi + hi), (bot, gr - hr, gi - hi)):
                put_right(m, 0, rows, jnp.concatenate([re[:, :HALF], im[:, :HALF]], axis=1))
                put_right(m, 1, rows, jnp.concatenate([re[:, HALF:], im[:, HALF:]], axis=1))
        tmp[m, 0] = mm(rop[m, 0], right_ref[0])
        tmp[m, 1] = mm(rop[m, 1], right_ref[1])
        for q in range(FRAME // CHUNK):
            rows = pl.ds(q * CHUNK, CHUNK)
            g, h = tmp[m, 0, rows, :], tmp[m, 1, rows, :]
            re = jnp.concatenate([g[:, :HALF] + h[:, :HALF], g[:, :HALF] - h[:, :HALF]], axis=1)
            im = jnp.concatenate([g[:, HALF:] + h[:, HALF:], g[:, HALF:] - h[:, HALF:]], axis=1)
            consume(m, rows, re, im)

    @pl.loop(0, 2)
    def _(f):
        r, c, r8, cs = corner(f)
        row_shift = r - r8
        col_shift = c - cs * HALF
        for copy in window_copies(f):
            copy.wait()

        for s in range(SLICES):
            for p in range(2):
                for q in range(FRAME // CHUNK):
                    x = win[f, s, p, pl.ds(q * CHUNK, CHUNK + 8), :]
                    x = pltpu.roll(x, lax.rem(WIN_COLS - col_shift, WIN_COLS), 1)[:, :FRAME]
                    x = pltpu.roll(x, lax.rem(CHUNK + 8 - row_shift, CHUNK + 8), 0)
                    obj[s, p, pl.ds(q * CHUNK, CHUNK), :] = x[:CHUNK]

        def enter(m, rows):
            pr, pi = probe_ref[m, 0, rows, :], probe_ref[m, 1, rows, :]
            a, b = obj[0, 0, rows, :], obj[0, 1, rows, :]
            return pr * a - pi * b, pr * b + pi * a

        def through(m, rows):
            ur, ui = u1[m, 0, rows, :], u1[m, 1, rows, :]
            a, b = obj[1, 0, rows, :], obj[1, 1, rows, :]
            return ur * a - ui * b, ur * b + ui * a

        def returning(m, rows):
            hr, hi = wave[m, 0, rows, :], wave[m, 1, rows, :]
            a, b = obj[1, 0, rows, :], obj[1, 1, rows, :]
            return hr * a + hi * b, hi * a - hr * b

        def propagator(rows, re, im):
            kr, ki = kern[0, rows, :], kern[1, rows, :]
            return re * kr - im * ki, re * ki + im * kr

        def adjoint(rows, re, im):
            kr, ki = kern[0, rows, :], kern[1, rows, :]
            return re * kr + im * ki, im * kr - re * ki

        def weighted(rows, re, im):
            w = cnt[f, rows, :]
            return re * w, im * w

        def keep_u1(m, rows, re, im):
            u1[m, 0, rows, :] = re
            u1[m, 1, rows, :] = im

        def keep_wave(m, rows, re, im):
            wave[m, 0, rows, :] = re
            wave[m, 1, rows, :] = im

        def scatter(s, source):
            for q in range(FRAME // CHUNK):
                rows = pl.ds(q * CHUNK, CHUNK)
                target = pl.ds(pl.multiple_of(r8 + q * CHUNK, 8), CHUNK + 8)
                gr = gi = None
                for m in range(MODES):
                    ur, ui = source(m, rows)
                    hr, hi = wave[m, 0, rows, :], wave[m, 1, rows, :]
                    tr, ti = ur * hr + ui * hi, ur * hi - ui * hr
                    gr, gi = (tr, ti) if gr is None else (gr + tr, gi + ti)
                below = jnp.zeros((8, FRAME), F32)
                beside = jnp.zeros((CHUNK + 8, HALF), F32)
                for p, g in enumerate((gr, gi)):
                    tall = pltpu.roll(jnp.concatenate([g, below], axis=0), row_shift, 0)
                    wide = pltpu.roll(jnp.concatenate([tall, beside], axis=1), col_shift, 1)
                    for j in range(3):
                        grad_ref[cs + j, s, p, target, :] += wide[:, j * HALF:(j + 1) * HALF]

        for m in range(MODES):
            forward(m, enter)
        for m in range(MODES):
            backward(m, propagator, keep_u1)
        for m in range(MODES):
            forward(m, through)
        for parity in range(2):
            for q in range(HALF // CHUNK):
                top = pl.ds(q * CHUNK, CHUNK)
                bot = pl.ds(HALF + q * CHUNK, CHUNK)
                rows = pl.ds(parity * HALF + q * CHUNK, CHUNK)
                level = bg[rows, :]
                for m in range(MODES):
                    re, im = freq[m, parity, top, :], freq[m, parity, bot, :]
                    level = level + re * re + im * im
                cnt[f, rows, :] = 1.0 - cnt[f, rows, :] / level
        for m in range(MODES):
            backward(m, weighted, keep_wave)
        scatter(1, lambda m, rows: (u1[m, 0, rows, :], u1[m, 1, rows, :]))
        for m in range(MODES):
            forward(m, returning)
        for m in range(MODES):
            backward(m, adjoint, keep_wave)
        scatter(0, lambda m, rows: (probe_ref[m, 0, rows, :], probe_ref[m, 1, rows, :]))
        for m in range(MODES):
            for q in range(FRAME // CHUNK):
                rows = pl.ds(q * CHUNK, CHUNK)
                hr, hi = wave[m, 0, rows, :], wave[m, 1, rows, :]
                a, b = obj[0, 0, rows, :], obj[0, 1, rows, :]
                tr, ti = hr * a + hi * b, hi * a - hr * b

                @pl.when(f == 0)
                def _():
                    probe_out_ref[m, 0, rows, :] = tr
                    probe_out_ref[m, 1, rows, :] = ti

                @pl.when(f != 0)
                def _():
                    probe_out_ref[m, 0, rows, :] += tr
                    probe_out_ref[m, 1, rows, :] += ti


def frame_terms(positions, ext, probe_modes, prop_phase, background, counts):
    lefts, rights, perms = dft_constants()
    vmem = pl.BlockSpec(memory_space=pltpu.VMEM)
    square = (FRAME, FRAME)
    return pl.pallas_call(
        frame_kernel,
        out_shape=(
            jax.ShapeDtypeStruct((STRIPS, SLICES, 2, ROWS_EXT, HALF), F32),
            jax.ShapeDtypeStruct((MODES, 2) + square, F32),
        ),
        in_specs=[pl.BlockSpec(memory_space=pltpu.SMEM), pl.BlockSpec(memory_space=pl.ANY)] + [vmem] * 7,
        out_specs=(vmem, vmem),
        scratch_shapes=[
            pltpu.VMEM((2, SLICES, 2, WIN_ROWS, WIN_COLS), F32),
            pltpu.VMEM((SLICES, 2) + square, F32),
            pltpu.VMEM((2,) + square, F32),
            pltpu.VMEM(square, F32),
            pltpu.VMEM((2,) + square, F32),
            pltpu.VMEM((MODES, 2) + square, F32),
            pltpu.VMEM((MODES, 2) + square, F32),
            pltpu.VMEM((MODES, 2, FRAME, 3 * FRAME), BF16),
            pltpu.VMEM((MODES, 2, 3 * FRAME, FRAME), BF16),
            pltpu.VMEM((MODES, 2) + square, F32),
            pltpu.VMEM((MODES, 2) + square, F32),
            pltpu.SemaphoreType.DMA((2, 3)),
        ],
        compiler_params=pltpu.CompilerParams(vmem_limit_bytes=48 << 20),
        name="frame_terms",
    )(positions, ext, probe_modes, prop_phase, background, counts,
      jnp.asarray(lefts), jnp.asarray(rights), jnp.asarray(perms))


MESH = pl.DeviceIdType.MESH


class Place:
    def __init__(self):
        tile, frame = lax.axis_index("tile"), lax.axis_index("frame")
        self.y, self.zl, self.core = tile // 4, (tile // 2) % 2, tile % 2
        self.zh, self.x = frame // 4, frame % 4
        self.z = self.zh * 2 + self.zl

    def at(self, y=None, zl=None, core=None, zh=None, x=None):
        pick = lambda given, own: own if given is None else given
        tile = (pick(y, self.y) * 2 + pick(zl, self.zl)) * 2 + pick(core, self.core)
        return tile, pick(zh, self.zh) * 4 + pick(x, self.x)

    def along_x(self, k):
        return self.at(x=(self.x + k) % 4)

    def along_y(self, k):
        return self.at(y=(self.y + k) % 4)

    def in_plane(self, j):
        q = (self.z * 4 + self.x + j) % 16
        z = q // 4
        return q, self.at(zl=z % 2, zh=z // 2, x=q % 4)

    def z_peer(self):
        return self.at(zh=1 - self.zh)

    def sibling(self):
        return self.at(core=1 - self.core)

    def outer(self):
        turn = self.core * self.zl + (1 - self.core) * (1 - self.zl)
        step = turn * (2 * self.core - 1)
        zh = turn * (1 - self.zh) + (1 - turn) * self.zh
        return self.at(y=(self.y + step + 4) % 4, zl=1 - self.zl, core=1 - self.core, zh=zh)


def greet(peers):
    barrier = pltpu.get_barrier_semaphore()
    for peer in peers:
        pl.semaphore_signal(barrier, inc=1, device_id=peer, device_id_type=MESH)
    pl.semaphore_wait(barrier, len(peers))


class Sender:
    def __init__(self, send_sems, recv_sems):
        self.send_sems, self.recv_sems = send_sems, recv_sems
        self.started = []

    def copy(self, src, dst, peer):
        n = len(self.started)
        made = pltpu.make_async_remote_copy(
            src_ref=src, dst_ref=dst, send_sem=self.send_sems.at[n], recv_sem=self.recv_sems.at[n],
            device_id=peer, device_id_type=MESH,
        )
        made.start()
        self.started.append(made)
        return made

    def finish(self):
        for made in self.started:
            made.wait_send()


def aligned(row):
    return pl.multiple_of(row, 8)


GATHER_COPIES = 2 * (4 + 3 + 16)


def gather_kernel(own_ref, ext_ref, local_sem, send_sems, recv_sems):
    me = Place()
    f, zf = me.zh * 4 + me.x, (1 - me.zh) * 4 + me.x
    sibling, outer, z_peer = me.sibling(), me.outer(), me.z_peer()
    across = [me.along_x(k) for k in (1, 2, 3)]
    greet([sibling, outer, z_peer] + across)
    send = Sender(send_sems, recv_sems)
    mine = pl.ds(HALO, FRAME)
    out_src, out_dst = aligned(HALO + HALO * me.core), aligned(384 * (1 - me.core))
    sib_src, sib_dst = aligned(HALO + HALO * (1 - me.core)), aligned(384 * me.core)
    edges = []

    def pass_edges(strip, s, ref=None):
        base = ext_ref.at[strip, s] if ref is None else ref.at[s]
        shift = 0 if ref is None else HALO
        edges.append(send.copy(base.at[:, pl.ds(aligned(out_src - shift), HALO), :], ext_ref.at[strip, s, :, pl.ds(out_dst, HALO), :], outer))
        edges.append(send.copy(base.at[:, pl.ds(aligned(sib_src - shift), HALO), :], ext_ref.at[strip, s, :, pl.ds(sib_dst, HALO), :], sibling))

    keep = pltpu.make_async_copy(own_ref, ext_ref.at[f, :, :, mine, :], local_sem)
    keep.start()
    first = {}
    for s in range(SLICES):
        first[s, 0] = send.copy(own_ref.at[s], ext_ref.at[f, s, :, mine, :], z_peer)
        for k in (1, 3, 2):
            first[s, k] = send.copy(own_ref.at[s], ext_ref.at[f, s, :, mine, :], across[k - 1])
    for s in range(SLICES):
        pass_edges(f, s, own_ref)
    second = {}
    for s in range(SLICES):
        first[s, 0].wait_recv()
        for k in (1, 3, 2):
            second[s, k] = send.copy(ext_ref.at[zf, s, :, mine, :], ext_ref.at[zf, s, :, mine, :], across[k - 1])
        pass_edges(zf, s)
    for batch, half in ((first, me.zh), (second, 1 - me.zh)):
        for s in range(SLICES):
            for k in (1, 3, 2):
                batch[s, k].wait_recv()
                pass_edges(half * 4 + (me.x + 4 - k) % 4, s)
    for made in edges:
        made.wait_recv()
    keep.wait()
    send.finish()


def gather_windows_rows(own):
    any_space = pl.BlockSpec(memory_space=pl.ANY)
    return pl.pallas_call(
        gather_kernel,
        out_shape=jax.ShapeDtypeStruct((STRIPS, SLICES, 2, ROWS_EXT, HALF), F32),
        in_specs=[any_space],
        out_specs=any_space,
        scratch_shapes=[
            pltpu.SemaphoreType.DMA(()),
            pltpu.SemaphoreType.DMA((GATHER_COPIES,)),
            pltpu.SemaphoreType.DMA((GATHER_COPIES,)),
        ],
        compiler_params=pltpu.CompilerParams(collective_id=1, has_side_effects=True),
        name="gather_strips",
    )(own)


SCATTER_COPIES = 32 + 12 + 2 + 1 + 3 + 15 + 15 + 3 + 1


def scatter_kernel(
    g_ref, p_ref, out_ref, pout_ref,
    edge_out, edge_sib, acc, xb, part, zb, sb, ph, yb, pq, xzb, send_sems, recv_sems,
):
    me = Place()
    sibling, outer, z_peer = me.sibling(), me.outer(), me.z_peer()
    across = [me.along_x(k) for k in (1, 2, 3)]
    upward = [me.along_y(k) for k in (1, 2, 3)]
    plane = [me.in_plane(j) for j in range(1, 16)]
    greet([sibling, outer] + upward + [peer for _, peer in plane])
    send = Sender(send_sems, recv_sems)
    out_src, sib_src = aligned(384 * me.core), aligned(384 * (1 - me.core))
    out_rows, sib_rows = aligned(HALO * me.core), aligned(HALO * (1 - me.core))
    order = [(s, k) for s in (1, 0) for k in (2, 1, 3, 0)]

    def strip(half, k):
        return half * 4 + (me.x + k) % 4

    edges = {}
    for s, k in order:
        for h in range(2):
            i = strip(h, k)
            edges[s, k, h, 0] = send.copy(g_ref.at[i, s, :, pl.ds(out_src, HALO), :], edge_out.at[s, k, h], outer)
            edges[s, k, h, 1] = send.copy(g_ref.at[i, s, :, pl.ds(sib_src, HALO), :], edge_sib.at[s, k, h], sibling)
        if (s, k) == order[0]:
            other = send.copy(p_ref.at[1 - me.core], sb, sibling)

    crossing = {}

    def take_edges(s, k):
        for h in range(2):
            edges[s, k, h, 0].wait_recv()
            edges[s, k, h, 1].wait_recv()
            i = strip(h, k)
            for c in range(2):
                acc[s, k, h, c, pl.ds(out_rows, HALO), :] = (
                    g_ref[i, s, c, pl.ds(aligned(HALO + out_rows), HALO), :] + edge_out[s, k, h, c]
                )
                acc[s, k, h, c, pl.ds(sib_rows, HALO), :] = (
                    g_ref[i, s, c, pl.ds(aligned(HALO + sib_rows), HALO), :] + edge_sib[s, k, h, c]
                )
            if k != 0:
                crossing[s, k, h] = send.copy(acc.at[s, k, h], xb.at[s, k - 1, h], across[k - 1])

    take_edges(1, 2)
    other.wait_recv()
    ph[...] = p_ref[me.core] + sb[...]
    quarter = lambda y: pl.ds(aligned(64 * y), 64)
    y_sums = [send.copy(ph.at[:, quarter((me.y + k) % 4), :], yb.at[k - 1], upward[k - 1]) for k in (1, 2, 3)]
    take_edges(1, 1)
    take_edges(1, 3)
    for made in y_sums:
        made.wait_recv()
    pq[...] = ph[:, quarter(me.y), :] + yb[0] + yb[1] + yb[2]
    spot = lambda q: (q // 8, pl.ds(aligned(8 * (q % 8)), 8))
    plane_sums = []
    for j, (q, peer) in enumerate(plane):
        c, rows = spot(q)
        plane_sums.append(send.copy(pq.at[c, rows, :], xzb.at[j], peer))
    take_edges(1, 0)
    take_edges(0, 2)
    for made in plane_sums:
        made.wait_recv()
    q = me.z * 4 + me.x
    c, rows = spot(q)
    total = pq[c, rows, :]
    for j in range(15):
        total = total + xzb[j]
    final_rows = pl.ds(aligned(64 * me.y + 8 * (q % 8)), 8)
    pout_ref[me.core, c, final_rows, :] = total
    plane_gather = [
        send.copy(pout_ref.at[me.core, c, final_rows, :], pout_ref.at[me.core, c, final_rows, :], peer)
        for _, peer in plane
    ]
    take_edges(0, 1)
    take_edges(0, 3)
    for made in plane_gather:
        made.wait_recv()
    mine = pout_ref.at[me.core, :, quarter(me.y), :]
    y_gather = [send.copy(mine, mine, peer) for peer in upward]
    take_edges(0, 0)

    last = {}
    for s in (1, 0):
        for k in (2, 1, 3):
            for h in range(2):
                crossing[s, k, h].wait_recv()
        for h in range(2):
            for c in range(2):
                part[s, h, c] = acc[s, 0, h, c] + xb[s, 0, h, c] + xb[s, 1, h, c] + xb[s, 2, h, c]
        last[s] = send.copy(part.at[s, 1 - me.zh], zb.at[s], z_peer)
        if s == 1:
            for made in y_gather:
                made.wait_recv()
            final = send.copy(pout_ref.at[me.core], pout_ref.at[me.core], sibling)
    for s in (1, 0):
        last[s].wait_recv()
        out_ref[s] = part[s, me.zh] + zb[s]
    final.wait_recv()
    send.finish()


def scatter_sums(grads, probe_term):
    vmem = pl.BlockSpec(memory_space=pltpu.VMEM)
    half_strip = (2, HALO, HALF)
    full_strip = (2, FRAME, HALF)
    return pl.pallas_call(
        scatter_kernel,
        out_shape=(
            jax.ShapeDtypeStruct((SLICES,) + full_strip, F32),
            jax.ShapeDtypeStruct((MODES, 2, FRAME, FRAME), F32),
        ),
        in_specs=[vmem, vmem],
        out_specs=(vmem, vmem),
        scratch_shapes=[
            pltpu.VMEM((2, 4, 2) + half_strip, F32),
            pltpu.VMEM((2, 4, 2) + half_strip, F32),
            pltpu.VMEM((2, 4, 2) + full_strip, F32),
            pltpu.VMEM((2, 3, 2) + full_strip, F32),
            pltpu.VMEM((2, 2) + full_strip, F32),
            pltpu.VMEM((2,) + full_strip, F32),
            pltpu.VMEM((2, FRAME, FRAME), F32),
            pltpu.VMEM((2, FRAME, FRAME), F32),
            pltpu.VMEM((3, 2, 64, FRAME), F32),
            pltpu.VMEM((2, 64, FRAME), F32),
            pltpu.VMEM((15, 8, FRAME), F32),
            pltpu.SemaphoreType.DMA((SCATTER_COPIES,)),
            pltpu.SemaphoreType.DMA((SCATTER_COPIES,)),
        ],
        compiler_params=pltpu.CompilerParams(collective_id=2, has_side_effects=True, vmem_limit_bytes=48 << 20),
        name="scatter_sums",
    )(grads, probe_term)


def shards(object_slices, probe_modes, prop_phase, background, positions, counts):
    ext = gather_windows_rows(object_slices)
    grads, probe_term = frame_terms(positions, ext, probe_modes, prop_phase, background, counts)
    return scatter_sums(grads, probe_term)


def solution(mesh):
    in_specs = (
        P(None, None, "tile", "frame"),
        P(),
        P(),
        P(),
        P(("tile", "frame"), None),
        P(("tile", "frame"), None, None),
    )
    out_specs = (P(None, None, "tile", "frame"), P())
    return jax.shard_map(shards, mesh=mesh, in_specs=in_specs, out_specs=out_specs, check_vma=False)
```

```python
import numpy as np
import ml_dtypes
import jax
import jax.numpy as jnp
from jax import lax
from jax.experimental import pallas as pl
from jax.experimental.pallas import tpu as pltpu
from jax.sharding import PartitionSpec as P

FRAME = 256
HALF = 128
SLICES = 2
MODES = 2
HALO = 128
ROWS_EXT = 512
STRIPS = 8
WIN_ROWS = 264
WIN_COLS = 384
CHUNK = 32
F32 = jnp.float32
BF16 = jnp.bfloat16


def dft_constants():
    k = np.arange(HALF)[:, None]
    n = np.arange(HALF)[None, :]
    mats = []
    for odd in (0, 1):
        turns = ((2 * k + odd) * n) % FRAME
        angle = -2.0 * np.pi * turns / FRAME
        c, s = np.cos(angle) / 16.0, np.sin(angle) / 16.0
        mats.append(np.block([[c, -s], [s, c]]))
    even, odd = mats
    lefts, rights = [], []
    for m in (even, odd, even.T, odd.T):
        hi = m.astype(ml_dtypes.bfloat16)
        lo = (m - hi.astype(np.float64)).astype(ml_dtypes.bfloat16)
        lefts.append(np.concatenate([hi, hi, lo], axis=1))
        rights.append(np.concatenate([hi, hi, lo], axis=0))
    perm = np.zeros((FRAME, FRAME))
    order = np.concatenate([np.arange(0, FRAME, 2), np.arange(1, FRAME, 2)])
    perm[np.arange(FRAME), order] = 1.0
    perms = np.stack([perm, perm.T]).astype(ml_dtypes.bfloat16)
    return np.stack(lefts), np.stack(rights), perms


def mm(a, b):
    return jnp.dot(a, b, preferred_element_type=F32)


def parts3(x):
    a = x.astype(BF16)
    r = x - a.astype(F32)
    b = r.astype(BF16)
    c = (r - b.astype(F32)).astype(BF16)
    return a, b, c


def reorder_exact(x, perm, perm_t):
    a, b, c = parts3(x)
    y = mm(perm, a) + mm(perm, b) + mm(perm, c)
    a, b, c = parts3(y)
    return mm(a, perm_t) + mm(b, perm_t) + mm(c, perm_t)


def frame_kernel(
    pos_ref, ext_ref, probe_ref, phase_ref, back_ref, counts_ref, left_ref, right_ref, perm_ref,
    grad_ref, probe_out_ref,
    win, obj, kern, bg, cnt, wave, u1, rop, lop, tmp, freq, win_sems,
):
    def corner(f):
        r = pos_ref[f, 0]
        c = pos_ref[f, 1]
        r8 = jnp.minimum(r // 8, 31) * 8
        cs = jnp.minimum(c // HALF, 5)
        return r, c, pl.multiple_of(r8, 8), cs

    def window_copies(f):
        _, _, r8, cs = corner(f)
        return [
            pltpu.make_async_copy(
                ext_ref.at[cs + j, :, :, pl.ds(r8, WIN_ROWS), :],
                win.at[f, :, :, :, pl.ds(j * HALF, HALF)],
                win_sems.at[f, j],
            )
            for j in range(3)
        ]

    for f in range(2):
        for copy in window_copies(f):
            copy.start()

    perm, perm_t = perm_ref[0], perm_ref[1]
    bg[...] = reorder_exact(back_ref[...], perm, perm_t)
    phase = reorder_exact(phase_ref[...], perm, perm_t)
    kern[0] = jnp.cos(phase)
    kern[1] = jnp.sin(phase)
    for f in range(2):
        half = mm(perm, counts_ref[f].astype(F32).astype(BF16)).astype(BF16)
        cnt[f] = mm(half, perm_t)

    grad_ref[...] = jnp.zeros_like(grad_ref)

    def put_right(m, parity, rows, x):
        hi = x.astype(BF16)
        lo = (x - hi.astype(F32)).astype(BF16)
        rop[m, parity, rows, 0:256] = hi
        rop[m, parity, rows, 256:512] = lo
        rop[m, parity, rows, 512:768] = hi

    def put_left(m, parity, start, x):
        hi = x.astype(BF16)
        lo = (x - hi.astype(F32)).astype(BF16)
        n = x.shape[0]
        lop[m, parity, pl.ds(start, n), :] = hi
        lop[m, parity, pl.ds(256 + start, n), :] = lo
        lop[m, parity, pl.ds(512 + start, n), :] = hi

    def forward(m, produce):
        for q in range(FRAME // CHUNK):
            rows = pl.ds(q * CHUNK, CHUNK)
            re, im = produce(m, rows)
            a, b = re[:, :HALF], re[:, HALF:]
            c, d = im[:, :HALF], im[:, HALF:]
            put_right(m, 0, rows, jnp.concatenate([a + b, c + d], axis=1))
            put_right(m, 1, rows, jnp.concatenate([a - b, c - d], axis=1))
        tmp[m, 0] = mm(rop[m, 0], right_ref[2])
        tmp[m, 1] = mm(rop[m, 1], right_ref[3])
        for q in range(HALF // CHUNK):
            top = pl.ds(q * CHUNK, CHUNK)
            bot = pl.ds(HALF + q * CHUNK, CHUNK)
            et, eb = tmp[m, 0, top, :], tmp[m, 0, bot, :]
            ot, ob = tmp[m, 1, top, :], tmp[m, 1, bot, :]
            for parity, e, o in ((0, et + eb, ot + ob), (1, et - eb, ot - ob)):
                put_left(m, parity, q * CHUNK, jnp.concatenate([e[:, :HALF], o[:, :HALF]], axis=1))
                put_left(m, parity, HALF + q * CHUNK, jnp.concatenate([e[:, HALF:], o[:, HALF:]], axis=1))
        freq[m, 0] = mm(left_ref[0], lop[m, 0])
        freq[m, 1] = mm(left_ref[1], lop[m, 1])

    def backward(m, modify, consume):
        for parity in range(2):
            for q in range(HALF // CHUNK):
                top = pl.ds(q * CHUNK, CHUNK)
                bot = pl.ds(HALF + q * CHUNK, CHUNK)
                table_rows = pl.ds(parity * HALF + q * CHUNK, CHUNK)
                re, im = modify(table_rows, freq[m, parity, top, :], freq[m, parity, bot, :])
                put_left(m, parity, q * CHUNK, re)
                put_left(m, parity, HALF + q * CHUNK, im)
        tmp[m, 0] = mm(left_ref[2], lop[m, 0])
        tmp[m, 1] = mm(left_ref[3], lop[m, 1])
        for q in range(HALF // CHUNK):
            top = pl.ds(q * CHUNK, CHUNK)
            bot = pl.ds(HALF + q * CHUNK, CHUNK)
            gr, gi = tmp[m, 0, top, :], tmp[m, 0, bot, :]
            hr, hi = tmp[m, 1, top, :], tmp[m, 1, bot, :]
            for rows, re, im in ((top, gr + hr, gi + hi), (bot, gr - hr, gi - hi)):
                put_right(m, 0, rows, jnp.concatenate([re[:, :HALF], im[:, :HALF]], axis=1))
                put_right(m, 1, rows, jnp.concatenate([re[:, HALF:], im[:, HALF:]], axis=1))
        tmp[m, 0] = mm(rop[m, 0], right_ref[0])
        tmp[m, 1] = mm(rop[m, 1], right_ref[1])
        for q in range(FRAME // CHUNK):
            rows = pl.ds(q * CHUNK, CHUNK)
            g, h = tmp[m, 0, rows, :], tmp[m, 1, rows, :]
            re = jnp.concatenate([g[:, :HALF] + h[:, :HALF], g[:, :HALF] - h[:, :HALF]], axis=1)
            im = jnp.concatenate([g[:, HALF:] + h[:, HALF:], g[:, HALF:] - h[:, HALF:]], axis=1)
            consume(m, rows, re, im)

    @pl.loop(0, 2)
    def _(f):
        r, c, r8, cs = corner(f)
        row_shift = r - r8
        col_shift = c - cs * HALF
        for copy in window_copies(f):
            copy.wait()

        for s in range(SLICES):
            for p in range(2):
                for q in range(FRAME // CHUNK):
                    x = win[f, s, p, pl.ds(q * CHUNK, CHUNK + 8), :]
                    x = pltpu.roll(x, lax.rem(WIN_COLS - col_shift, WIN_COLS), 1)[:, :FRAME]
                    x = pltpu.roll(x, lax.rem(CHUNK + 8 - row_shift, CHUNK + 8), 0)
                    obj[s, p, pl.ds(q * CHUNK, CHUNK), :] = x[:CHUNK]

        def enter(m, rows):
            pr, pi = probe_ref[m, 0, rows, :], probe_ref[m, 1, rows, :]
            a, b = obj[0, 0, rows, :], obj[0, 1, rows, :]
            return pr * a - pi * b, pr * b + pi * a

        def through(m, rows):
            ur, ui = u1[m, 0, rows, :], u1[m, 1, rows, :]
            a, b = obj[1, 0, rows, :], obj[1, 1, rows, :]
            return ur * a - ui * b, ur * b + ui * a

        def returning(m, rows):
            hr, hi = wave[m, 0, rows, :], wave[m, 1, rows, :]
            a, b = obj[1, 0, rows, :], obj[1, 1, rows, :]
            return hr * a + hi * b, hi * a - hr * b

        def propagator(rows, re, im):
            kr, ki = kern[0, rows, :], kern[1, rows, :]
            return re * kr - im * ki, re * ki + im * kr

        def adjoint(rows, re, im):
            kr, ki = kern[0, rows, :], kern[1, rows, :]
            return re * kr + im * ki, im * kr - re * ki

        def weighted(rows, re, im):
            w = cnt[f, rows, :]
            return re * w, im * w

        def keep_u1(m, rows, re, im):
            u1[m, 0, rows, :] = re
            u1[m, 1, rows, :] = im

        def keep_wave(m, rows, re, im):
            wave[m, 0, rows, :] = re
            wave[m, 1, rows, :] = im

        def scatter(s, source):
            for q in range(FRAME // CHUNK):
                rows = pl.ds(q * CHUNK, CHUNK)
                target = pl.ds(pl.multiple_of(r8 + q * CHUNK, 8), CHUNK + 8)
                gr = gi = None
                for m in range(MODES):
                    ur, ui = source(m, rows)
                    hr, hi = wave[m, 0, rows, :], wave[m, 1, rows, :]
                    tr, ti = ur * hr + ui * hi, ur * hi - ui * hr
                    gr, gi = (tr, ti) if gr is None else (gr + tr, gi + ti)
                below = jnp.zeros((8, FRAME), F32)
                beside = jnp.zeros((CHUNK + 8, HALF), F32)
                for p, g in enumerate((gr, gi)):
                    tall = pltpu.roll(jnp.concatenate([g, below], axis=0), row_shift, 0)
                    wide = pltpu.roll(jnp.concatenate([tall, beside], axis=1), col_shift, 1)
                    for j in range(3):
                        grad_ref[cs + j, s, p, target, :] += wide[:, j * HALF:(j + 1) * HALF]

        for m in range(MODES):
            forward(m, enter)
        for m in range(MODES):
            backward(m, propagator, keep_u1)
        for m in range(MODES):
            forward(m, through)
        for parity in range(2):
            for q in range(HALF // CHUNK):
                top = pl.ds(q * CHUNK, CHUNK)
                bot = pl.ds(HALF + q * CHUNK, CHUNK)
                rows = pl.ds(parity * HALF + q * CHUNK, CHUNK)
                level = bg[rows, :]
                for m in range(MODES):
                    re, im = freq[m, parity, top, :], freq[m, parity, bot, :]
                    level = level + re * re + im * im
                cnt[f, rows, :] = 1.0 - cnt[f, rows, :] / level
        for m in range(MODES):
            backward(m, weighted, keep_wave)
        scatter(1, lambda m, rows: (u1[m, 0, rows, :], u1[m, 1, rows, :]))
        for m in range(MODES):
            forward(m, returning)
        for m in range(MODES):
            backward(m, adjoint, keep_wave)
        scatter(0, lambda m, rows: (probe_ref[m, 0, rows, :], probe_ref[m, 1, rows, :]))
        for m in range(MODES):
            for q in range(FRAME // CHUNK):
                rows = pl.ds(q * CHUNK, CHUNK)
                hr, hi = wave[m, 0, rows, :], wave[m, 1, rows, :]
                a, b = obj[0, 0, rows, :], obj[0, 1, rows, :]
                tr, ti = hr * a + hi * b, hi * a - hr * b

                @pl.when(f == 0)
                def _():
                    probe_out_ref[m, 0, rows, :] = tr
                    probe_out_ref[m, 1, rows, :] = ti

                @pl.when(f != 0)
                def _():
                    probe_out_ref[m, 0, rows, :] += tr
                    probe_out_ref[m, 1, rows, :] += ti


def frame_terms(positions, ext, probe_modes, prop_phase, background, counts):
    lefts, rights, perms = dft_constants()
    vmem = pl.BlockSpec(memory_space=pltpu.VMEM)
    square = (FRAME, FRAME)
    return pl.pallas_call(
        frame_kernel,
        out_shape=(
            jax.ShapeDtypeStruct((STRIPS, SLICES, 2, ROWS_EXT, HALF), F32),
            jax.ShapeDtypeStruct((MODES, 2) + square, F32),
        ),
        in_specs=[pl.BlockSpec(memory_space=pltpu.SMEM), pl.BlockSpec(memory_space=pl.ANY)] + [vmem] * 7,
        out_specs=(vmem, vmem),
        scratch_shapes=[
            pltpu.VMEM((2, SLICES, 2, WIN_ROWS, WIN_COLS), F32),
            pltpu.VMEM((SLICES, 2) + square, F32),
            pltpu.VMEM((2,) + square, F32),
            pltpu.VMEM(square, F32),
            pltpu.VMEM((2,) + square, F32),
            pltpu.VMEM((MODES, 2) + square, F32),
            pltpu.VMEM((MODES, 2) + square, F32),
            pltpu.VMEM((MODES, 2, FRAME, 3 * FRAME), BF16),
            pltpu.VMEM((MODES, 2, 3 * FRAME, FRAME), BF16),
            pltpu.VMEM((MODES, 2) + square, F32),
            pltpu.VMEM((MODES, 2) + square, F32),
            pltpu.SemaphoreType.DMA((2, 3)),
        ],
        compiler_params=pltpu.CompilerParams(vmem_limit_bytes=48 << 20),
        name="frame_terms",
    )(positions, ext, probe_modes, prop_phase, background, counts,
      jnp.asarray(lefts), jnp.asarray(rights), jnp.asarray(perms))


MESH = pl.DeviceIdType.MESH


class Place:
    def __init__(self):
        tile, frame = lax.axis_index("tile"), lax.axis_index("frame")
        self.y, self.zl, self.core = tile // 4, (tile // 2) % 2, tile % 2
        self.zh, self.x = frame // 4, frame % 4
        self.z = self.zh * 2 + self.zl

    def at(self, y=None, zl=None, core=None, zh=None, x=None):
        pick = lambda given, own: own if given is None else given
        tile = (pick(y, self.y) * 2 + pick(zl, self.zl)) * 2 + pick(core, self.core)
        return tile, pick(zh, self.zh) * 4 + pick(x, self.x)

    def along_x(self, k):
        return self.at(x=(self.x + k) % 4)

    def along_y(self, k):
        return self.at(y=(self.y + k) % 4)

    def in_plane(self, j):
        q = (self.z * 4 + self.x + j) % 16
        z = q // 4
        return q, self.at(zl=z % 2, zh=z // 2, x=q % 4)

    def z_peer(self):
        return self.at(zh=1 - self.zh)

    def sibling(self):
        return self.at(core=1 - self.core)

    def outer(self):
        turn = self.core * self.zl + (1 - self.core) * (1 - self.zl)
        step = turn * (2 * self.core - 1)
        zh = turn * (1 - self.zh) + (1 - turn) * self.zh
        return self.at(y=(self.y + step + 4) % 4, zl=1 - self.zl, core=1 - self.core, zh=zh)


def greet(peers):
    barrier = pltpu.get_barrier_semaphore()
    for peer in peers:
        pl.semaphore_signal(barrier, inc=1, device_id=peer, device_id_type=MESH)
    pl.semaphore_wait(barrier, len(peers))


class Sender:
    def __init__(self, send_sems, recv_sems):
        self.send_sems, self.recv_sems = send_sems, recv_sems
        self.started = []

    def copy(self, src, dst, peer):
        n = len(self.started)
        made = pltpu.make_async_remote_copy(
            src_ref=src, dst_ref=dst, send_sem=self.send_sems.at[n], recv_sem=self.recv_sems.at[n],
            device_id=peer, device_id_type=MESH,
        )
        made.start()
        self.started.append(made)
        return made

    def finish(self):
        for made in self.started:
            made.wait_send()


def aligned(row):
    return pl.multiple_of(row, 8)


GATHER_COPIES = 6 + 4 + 8 + 32


def gather_kernel(own_ref, ext_ref, local_sem, send_sems, recv_sems):
    me = Place()
    f, zf = me.zh * 4 + me.x, (1 - me.zh) * 4 + me.x
    sibling, outer, z_peer = me.sibling(), me.outer(), me.z_peer()
    ahead, behind = me.along_x(1), me.along_x(3)
    greet([sibling, outer, z_peer, ahead, behind])
    send = Sender(send_sems, recv_sems)
    mine = pl.ds(HALO, FRAME)
    out_src, out_dst = aligned(HALO + HALO * me.core), aligned(384 * (1 - me.core))
    sib_src, sib_dst = aligned(HALO + HALO * (1 - me.core)), aligned(384 * me.core)
    edges = []

    def pass_edges(strip, s, ref=None):
        base = ext_ref.at[strip, s] if ref is None else ref.at[s]
        shift = 0 if ref is None else HALO
        edges.append(send.copy(base.at[:, pl.ds(aligned(out_src - shift), HALO), :], ext_ref.at[strip, s, :, pl.ds(out_dst, HALO), :], outer))
        edges.append(send.copy(base.at[:, pl.ds(aligned(sib_src - shift), HALO), :], ext_ref.at[strip, s, :, pl.ds(sib_dst, HALO), :], sibling))

    keep = pltpu.make_async_copy(own_ref, ext_ref.at[f, :, :, mine, :], local_sem)
    keep.start()
    to_z, to_x, relayed = {}, {}, {}
    own_half, other_half = 0, 1
    half_of = (me.zh, 1 - me.zh)

    def strip_at(which, k):
        return half_of[which] * 4 + (me.x + k + 4) % 4

    for s in range(SLICES):
        to_z[s] = send.copy(own_ref.at[s], ext_ref.at[f, s, :, mine, :], z_peer)
        to_x[own_half, s, 0] = send.copy(own_ref.at[s], ext_ref.at[f, s, :, mine, :], ahead)
        to_x[own_half, s, 1] = send.copy(own_ref.at[s], ext_ref.at[f, s, :, mine, :], behind)
    for s in range(SLICES):
        pass_edges(f, s, own_ref)

    def from_z(s):
        to_z[s].wait_recv()
        whole = ext_ref.at[zf, s, :, mine, :]
        to_x[other_half, s, 0] = send.copy(whole, whole, ahead)
        to_x[other_half, s, 1] = send.copy(whole, whole, behind)
        pass_edges(zf, s)

    def from_x(which, s):
        for way, peer, k in ((0, ahead, -1), (1, behind, 1)):
            to_x[which, s, way].wait_recv()
            plane = ext_ref.at[strip_at(which, k), s, way, mine, :]
            relayed[which, s, way] = send.copy(plane, plane, peer)
        for k in (-1, 1):
            pass_edges(strip_at(which, k), s)

    def from_relay(which, s):
        for way in range(2):
            relayed[which, s, way].wait_recv()
        pass_edges(strip_at(which, 2), s)

    from_z(0)
    from_x(own_half, 0)
    from_z(1)
    from_x(own_half, 1)
    from_relay(own_half, 0)
    from_x(other_half, 0)
    from_relay(own_half, 1)
    from_x(other_half, 1)
    from_relay(other_half, 0)
    from_relay(other_half, 1)
    for made in edges:
        made.wait_recv()
    keep.wait()
    send.finish()


def gather_windows_rows(own):
    any_space = pl.BlockSpec(memory_space=pl.ANY)
    return pl.pallas_call(
        gather_kernel,
        out_shape=jax.ShapeDtypeStruct((STRIPS, SLICES, 2, ROWS_EXT, HALF), F32),
        in_specs=[any_space],
        out_specs=any_space,
        scratch_shapes=[
            pltpu.SemaphoreType.DMA(()),
            pltpu.SemaphoreType.DMA((GATHER_COPIES,)),
            pltpu.SemaphoreType.DMA((GATHER_COPIES,)),
        ],
        compiler_params=pltpu.CompilerParams(collective_id=1, has_side_effects=True),
        name="gather_strips",
    )(own)


SCATTER_COPIES = 32 + 8 + 16 + 2 + 1 + 3 + 15 + 15 + 3 + 1


def scatter_kernel(
    g_ref, p_ref, out_ref, pout_ref,
    edge_out, edge_sib, acc, rb, xb, part, zb, sb, ph, yb, pq, xzb, local_sems, send_sems, recv_sems,
):
    me = Place()
    sibling, outer, z_peer = me.sibling(), me.outer(), me.z_peer()
    ahead, behind = me.along_x(1), me.along_x(3)
    upward = [me.along_y(k) for k in (1, 2, 3)]
    plane = [me.in_plane(j) for j in range(1, 16)]
    greet([sibling, outer] + upward + [peer for _, peer in plane])
    send = Sender(send_sems, recv_sems)
    out_src, sib_src = aligned(384 * me.core), aligned(384 * (1 - me.core))
    out_rows, sib_rows = aligned(HALO * me.core), aligned(HALO * (1 - me.core))
    order = [(1, 2), (1, 1), (1, 3), (0, 2), (0, 1), (0, 3), (1, 0), (0, 0)]

    def strip(half, k):
        return half * 4 + (me.x + k) % 4

    local = {}
    for n, (s, k) in enumerate(order):
        for h in range(2):
            local[s, k, h] = pltpu.make_async_copy(
                g_ref.at[strip(h, k), s, :, pl.ds(HALO, FRAME), :], acc.at[s, k, h], local_sems.at[n, h]
            )
            local[s, k, h].start()
    edges = {}
    waiting = list(order)

    def start_edges():
        if waiting:
            s, k = waiting.pop(0)
            for h in range(2):
                i = strip(h, k)
                edges[s, k, h, 0] = send.copy(g_ref.at[i, s, :, pl.ds(out_src, HALO), :], edge_out.at[s, k, h], outer)
                edges[s, k, h, 1] = send.copy(g_ref.at[i, s, :, pl.ds(sib_src, HALO), :], edge_sib.at[s, k, h], sibling)

    start_edges()
    start_edges()
    other = send.copy(p_ref.at[1 - me.core], sb, sibling)
    start_edges()
    relays, crossing = {}, {}

    def take_edges(s, k):
        for h in range(2):
            local[s, k, h].wait()
            edges[s, k, h, 0].wait_recv()
            edges[s, k, h, 1].wait_recv()
            acc[s, k, h, :, pl.ds(out_rows, HALO), :] += edge_out[s, k, h]
            acc[s, k, h, :, pl.ds(sib_rows, HALO), :] += edge_sib[s, k, h]
        for h in range(2):
            if k == 2:
                relays[s, h, 0] = send.copy(acc.at[s, k, h, 0], rb.at[s, h, 0], ahead)
                relays[s, h, 1] = send.copy(acc.at[s, k, h, 1], rb.at[s, h, 1], behind)
            if k == 1:
                crossing[s, h, 0, 1] = send.copy(acc.at[s, k, h, 1], xb.at[s, h, 0, 1], ahead)
            if k == 3:
                crossing[s, h, 1, 0] = send.copy(acc.at[s, k, h, 0], xb.at[s, h, 1, 0], behind)
        start_edges()

    def take_relays(s):
        for h in range(2):
            for way, k, peer in ((0, 1, ahead), (1, 3, behind)):
                relays[s, h, way].wait_recv()
                acc[s, k, h, way] += rb[s, h, way]
                crossing[s, h, way, way] = send.copy(acc.at[s, k, h, way], xb.at[s, h, way, way], peer)

    take_edges(1, 2)
    other.wait_recv()
    ph[...] = p_ref[me.core] + sb[...]
    quarter = lambda y: pl.ds(aligned(64 * y), 64)
    y_sums = [send.copy(ph.at[:, quarter((me.y + k) % 4), :], yb.at[k - 1], upward[k - 1]) for k in (1, 2, 3)]
    take_edges(1, 1)
    take_edges(1, 3)
    for made in y_sums:
        made.wait_recv()
    pq[...] = ph[:, quarter(me.y), :] + yb[0] + yb[1] + yb[2]
    spot = lambda q: (q // 8, pl.ds(aligned(8 * (q % 8)), 8))
    plane_sums = []
    for j, (q, peer) in enumerate(plane):
        c, rows = spot(q)
        plane_sums.append(send.copy(pq.at[c, rows, :], xzb.at[j], peer))
    take_relays(1)
    take_edges(0, 2)
    for made in plane_sums:
        made.wait_recv()
    q = me.z * 4 + me.x
    c, rows = spot(q)
    total = pq[c, rows, :]
    for j in range(15):
        total = total + xzb[j]
    final_rows = pl.ds(aligned(64 * me.y + 8 * (q % 8)), 8)
    pout_ref[me.core, c, final_rows, :] = total
    plane_gather = [
        send.copy(pout_ref.at[me.core, c, final_rows, :], pout_ref.at[me.core, c, final_rows, :], peer)
        for _, peer in plane
    ]
    take_edges(0, 1)
    take_edges(0, 3)
    take_relays(0)
    take_edges(1, 0)
    for made in plane_gather:
        made.wait_recv()
    mine = pout_ref.at[me.core, :, quarter(me.y), :]
    y_gather = [send.copy(mine, mine, peer) for peer in upward]
    take_edges(0, 0)

    last = {}
    for s in (1, 0):
        for h in range(2):
            for way in range(2):
                for c in range(2):
                    crossing[s, h, way, c].wait_recv()
            part[s, h] = acc[s, 0, h] + xb[s, h, 0] + xb[s, h, 1]
        last[s] = send.copy(part.at[s, 1 - me.zh], zb.at[s], z_peer)
        if s == 1:
            for made in y_gather:
                made.wait_recv()
            final = send.copy(pout_ref.at[me.core], pout_ref.at[me.core], sibling)
    for s in (1, 0):
        last[s].wait_recv()
        out_ref[s] = part[s, me.zh] + zb[s]
    final.wait_recv()
    send.finish()


def scatter_sums(grads, probe_term):
    vmem = pl.BlockSpec(memory_space=pltpu.VMEM)
    half_strip = (2, HALO, HALF)
    full_strip = (2, FRAME, HALF)
    return pl.pallas_call(
        scatter_kernel,
        out_shape=(
            jax.ShapeDtypeStruct((SLICES,) + full_strip, F32),
            jax.ShapeDtypeStruct((MODES, 2, FRAME, FRAME), F32),
        ),
        in_specs=[pl.BlockSpec(memory_space=pl.ANY), vmem],
        out_specs=(vmem, vmem),
        scratch_shapes=[
            pltpu.VMEM((2, 4, 2) + half_strip, F32),
            pltpu.VMEM((2, 4, 2) + half_strip, F32),
            pltpu.VMEM((2, 4, 2) + full_strip, F32),
            pltpu.VMEM((2, 2, 2, FRAME, HALF), F32),
            pltpu.VMEM((2, 2, 2) + full_strip, F32),
            pltpu.VMEM((2, 2) + full_strip, F32),
            pltpu.VMEM((2,) + full_strip, F32),
            pltpu.VMEM((2, FRAME, FRAME), F32),
            pltpu.VMEM((2, FRAME, FRAME), F32),
            pltpu.VMEM((3, 2, 64, FRAME), F32),
            pltpu.VMEM((2, 64, FRAME), F32),
            pltpu.VMEM((15, 8, FRAME), F32),
            pltpu.SemaphoreType.DMA((8, 2)),
            pltpu.SemaphoreType.DMA((SCATTER_COPIES,)),
            pltpu.SemaphoreType.DMA((SCATTER_COPIES,)),
        ],
        compiler_params=pltpu.CompilerParams(collective_id=2, has_side_effects=True, vmem_limit_bytes=48 << 20),
        name="scatter_sums",
    )(grads, probe_term)


def shards(object_slices, probe_modes, prop_phase, background, positions, counts):
    ext = gather_windows_rows(object_slices)
    grads, probe_term = frame_terms(positions, ext, probe_modes, prop_phase, background, counts)
    return scatter_sums(grads, probe_term)


def solution(mesh):
    in_specs = (
        P(None, None, "tile", "frame"),
        P(),
        P(),
        P(),
        P(("tile", "frame"), None),
        P(("tile", "frame"), None, None),
    )
    out_specs = (P(None, None, "tile", "frame"), P())
    return jax.shard_map(shards, mesh=mesh, in_specs=in_specs, out_specs=out_specs, check_vma=False)
```

```python
import numpy as np
import ml_dtypes
import jax
import jax.numpy as jnp
from jax import lax
from jax.experimental import pallas as pl
from jax.experimental.pallas import tpu as pltpu
from jax.sharding import PartitionSpec as P

FRAME = 256
HALF = 128
SLICES = 2
MODES = 2
HALO = 128
ROWS_EXT = 512
STRIPS = 8
WIN_COLS = 384
CHUNK = 32
TALL = 88
BLANK_ROWS = 248
PAD_ROWS = 2 * BLANK_ROWS + 264
F32 = jnp.float32
BF16 = jnp.bfloat16


def dft_constants():
    k = np.arange(HALF)[:, None]
    n = np.arange(HALF)[None, :]
    mats = []
    for odd in (0, 1):
        turns = ((2 * k + odd) * n) % FRAME
        angle = -2.0 * np.pi * turns / FRAME
        c, s = np.cos(angle) / 16.0, np.sin(angle) / 16.0
        mats.append(np.block([[c, -s], [s, c]]))
    even, odd = mats
    lefts, rights = [], []
    for m in (even, odd, even.T, odd.T):
        hi = m.astype(ml_dtypes.bfloat16)
        lo = (m - hi.astype(np.float64)).astype(ml_dtypes.bfloat16)
        lefts.append(np.concatenate([hi, hi, lo], axis=1))
        rights.append(np.concatenate([hi, hi, lo], axis=0))
    perm = np.zeros((FRAME, FRAME))
    order = np.concatenate([np.arange(0, FRAME, 2), np.arange(1, FRAME, 2)])
    perm[np.arange(FRAME), order] = 1.0
    perms = np.stack([perm, perm.T]).astype(ml_dtypes.bfloat16)
    return np.stack(lefts), np.stack(rights), perms


def mm(a, b):
    return jnp.dot(a, b, preferred_element_type=F32)


def parts3(x):
    a = x.astype(BF16)
    r = x - a.astype(F32)
    b = r.astype(BF16)
    c = (r - b.astype(F32)).astype(BF16)
    return a, b, c


def reorder_exact(x, perm, perm_t):
    a, b, c = parts3(x)
    y = mm(perm, a) + mm(perm, b) + mm(perm, c)
    a, b, c = parts3(y)
    return mm(a, perm_t) + mm(b, perm_t) + mm(c, perm_t)


def corner(pos_ref, f):
    r, c = pos_ref[f, 0], pos_ref[f, 1]
    block = jnp.minimum(r // 8, 31)
    cs = jnp.minimum(c // HALF, 5)
    return block, r - block * 8, cs, c - cs * HALF


MESH = pl.DeviceIdType.MESH


class Place:
    def __init__(self):
        tile, frame = lax.axis_index("tile"), lax.axis_index("frame")
        self.y, self.zl, self.core = tile // 4, (tile // 2) % 2, tile % 2
        self.zh, self.x = frame // 4, frame % 4
        self.z = self.zh * 2 + self.zl

    def at(self, y=None, zl=None, core=None, zh=None, x=None):
        pick = lambda given, own: own if given is None else given
        tile = (pick(y, self.y) * 2 + pick(zl, self.zl)) * 2 + pick(core, self.core)
        return tile, pick(zh, self.zh) * 4 + pick(x, self.x)

    def along_x(self, k):
        return self.at(x=(self.x + k) % 4)

    def along_y(self, k):
        return self.at(y=(self.y + k) % 4)

    def in_plane(self, j):
        q = (self.z * 4 + self.x + j) % 16
        z = q // 4
        return q, self.at(zl=z % 2, zh=z // 2, x=q % 4)

    def z_peer(self):
        return self.at(zh=1 - self.zh)

    def sibling(self):
        return self.at(core=1 - self.core)

    def outer(self):
        turn = self.core * self.zl + (1 - self.core) * (1 - self.zl)
        step = turn * (2 * self.core - 1)
        zh = turn * (1 - self.zh) + (1 - turn) * self.zh
        return self.at(y=(self.y + step + 4) % 4, zl=1 - self.zl, core=1 - self.core, zh=zh)


def greet(peers):
    barrier = pltpu.get_barrier_semaphore()
    for peer in peers:
        pl.semaphore_signal(barrier, inc=1, device_id=peer, device_id_type=MESH)
    pl.semaphore_wait(barrier, len(peers))


class Sender:
    def __init__(self, send_sems, recv_sems):
        self.send_sems, self.recv_sems = send_sems, recv_sems
        self.started = []

    def copy(self, src, dst, peer):
        n = len(self.started)
        made = pltpu.make_async_remote_copy(
            src_ref=src, dst_ref=dst, send_sem=self.send_sems.at[n], recv_sem=self.recv_sems.at[n],
            device_id=peer, device_id_type=MESH,
        )
        made.start()
        self.started.append(made)
        return made

    def finish(self):
        for made in self.started:
            made.wait_send()


def aligned(row):
    return pl.multiple_of(row, 8)


GATHER_COPIES = 6 + 4 + 8 + 32
SCATTER_COPIES = 32 + 8 + 16 + 2 + 1 + 3 + 15 + 15 + 3 + 1
COPIES = GATHER_COPIES + SCATTER_COPIES


def gradient_kernel(
    pos_ref, own_ref, probe_in, phase_in, back_in, counts_in, left_in, right_in, perm_in,
    out_ref, pout_ref,
    ext_0, ext_1, g_0, g_1, probe, phase_raw, back_raw, counts_raw, left, right, perms,
    obj, kern, bg, cnt, wave, u1, rop, lop, tmp, freq, padded, placed,
    edge_out, edge_sib, rb, xb, part, zb, p_sum, sb, ph, yb, pq, xzb,
    local_sems, send_sems, recv_sems,
):
    exts, gs = (ext_0, ext_1), (g_0, g_1)
    me = Place()
    f_own, f_other = me.zh * 4 + me.x, (1 - me.zh) * 4 + me.x
    sibling, outer, z_peer = me.sibling(), me.outer(), me.z_peer()
    ahead, behind = me.along_x(1), me.along_x(3)
    upward = [me.along_y(k) for k in (1, 2, 3)]
    plane = [me.in_plane(j) for j in range(1, 16)]

    loads = [
        pltpu.make_async_copy(src, dst, local_sems.at[n])
        for n, (src, dst) in enumerate((
            (perm_in, perms), (back_in, back_raw), (phase_in, phase_raw), (counts_in, counts_raw),
            (probe_in, probe), (left_in, left), (right_in, right),
        ))
    ]
    for load in loads:
        load.start()
    mine, own_blocks = pl.ds(HALO, FRAME), pl.ds(16, 32)
    keeps = [
        pltpu.make_async_copy(own_ref.at[s], exts[s].at[f_own, :, own_blocks], local_sems.at[len(loads) + s])
        for s in range(SLICES)
    ]
    for keep in keeps:
        keep.start()

    greet([sibling, outer] + upward + [peer for _, peer in plane])
    send = Sender(send_sems, recv_sems)

    out_src, out_dst = 16 + 16 * me.core, 48 * (1 - me.core)
    sib_src, sib_dst = 16 + 16 * (1 - me.core), 48 * me.core
    margins = ([], [])

    def pass_edges(strip, s, ref=None):
        base = exts[s].at[strip] if ref is None else ref.at[s]
        shift = 0 if ref is None else 16
        for src, dst, peer in ((out_src, out_dst, outer), (sib_src, sib_dst, sibling)):
            margins[s].append(send.copy(
                base.at[:, pl.ds(src - shift, 16)], exts[s].at[strip, :, pl.ds(dst, 16)], peer
            ))

    to_z, to_x, relayed = {}, {}, {}
    own_half, other_half = 0, 1
    half_of = (me.zh, 1 - me.zh)

    def strip_at(which, k):
        return half_of[which] * 4 + (me.x + k + 4) % 4

    def own_to_z(s):
        to_z[s] = send.copy(own_ref.at[s], exts[s].at[f_own, :, own_blocks], z_peer)

    def own_to_x(s):
        to_x[own_half, s, 0] = send.copy(own_ref.at[s], exts[s].at[f_own, :, own_blocks], ahead)
        to_x[own_half, s, 1] = send.copy(own_ref.at[s], exts[s].at[f_own, :, own_blocks], behind)

    def from_z(s):
        to_z[s].wait_recv()
        whole = exts[s].at[f_other, :, own_blocks]
        to_x[other_half, s, 0] = send.copy(whole, whole, ahead)
        to_x[other_half, s, 1] = send.copy(whole, whole, behind)
        pass_edges(f_other, s)

    def from_x(which, s):
        for way, peer, k in ((0, ahead, -1), (1, behind, 1)):
            to_x[which, s, way].wait_recv()
            half = exts[s].at[strip_at(which, k), way, own_blocks]
            relayed[which, s, way] = send.copy(half, half, peer)
        for k in (-1, 1):
            pass_edges(strip_at(which, k), s)

    def from_relay(which, s):
        for way in range(2):
            relayed[which, s, way].wait_recv()
        pass_edges(strip_at(which, 2), s)

    def cut(s):
        keeps[s].wait()
        for made in margins[s]:
            made.wait_recv()

        @pl.loop(0, 2)
        def _(f):
            block, row_shift, cs, col_shift = corner(pos_ref, f)
            for p in range(2):
                for q in range(FRAME // CHUNK):
                    x = jnp.concatenate([
                        jnp.concatenate([exts[s][cs + j, p, block + q * CHUNK // 8 + n] for n in range(CHUNK // 8 + 1)], axis=0)
                        for j in range(3)
                    ], axis=1)
                    x = pltpu.roll(x, lax.rem(WIN_COLS - col_shift, WIN_COLS), 1)[:, :FRAME]
                    x = pltpu.roll(x, lax.rem(CHUNK + 8 - row_shift, CHUNK + 8), 0)
                    obj[f, s, p, pl.ds(q * CHUNK, CHUNK), :] = x[:CHUNK]

    def put_right(m, parity, rows, x):
        hi = x.astype(BF16)
        lo = (x - hi.astype(F32)).astype(BF16)
        rop[m, parity, rows, 0:256] = hi
        rop[m, parity, rows, 256:512] = lo
        rop[m, parity, rows, 512:768] = hi

    def put_left(m, parity, start, x):
        hi = x.astype(BF16)
        lo = (x - hi.astype(F32)).astype(BF16)
        n = x.shape[0]
        lop[m, parity, pl.ds(start, n), :] = hi
        lop[m, parity, pl.ds(256 + start, n), :] = lo
        lop[m, parity, pl.ds(512 + start, n), :] = hi

    def forward(m, produce):
        for q in range(FRAME // CHUNK):
            rows = pl.ds(q * CHUNK, CHUNK)
            re, im = produce(m, rows)
            a, b = re[:, :HALF], re[:, HALF:]
            c, d = im[:, :HALF], im[:, HALF:]
            put_right(m, 0, rows, jnp.concatenate([a + b, c + d], axis=1))
            put_right(m, 1, rows, jnp.concatenate([a - b, c - d], axis=1))
        tmp[m, 0] = mm(rop[m, 0], right[2])
        tmp[m, 1] = mm(rop[m, 1], right[3])
        for q in range(HALF // CHUNK):
            top = pl.ds(q * CHUNK, CHUNK)
            bot = pl.ds(HALF + q * CHUNK, CHUNK)
            et, eb = tmp[m, 0, top, :], tmp[m, 0, bot, :]
            ot, ob = tmp[m, 1, top, :], tmp[m, 1, bot, :]
            for parity, e, o in ((0, et + eb, ot + ob), (1, et - eb, ot - ob)):
                put_left(m, parity, q * CHUNK, jnp.concatenate([e[:, :HALF], o[:, :HALF]], axis=1))
                put_left(m, parity, HALF + q * CHUNK, jnp.concatenate([e[:, HALF:], o[:, HALF:]], axis=1))
        freq[m, 0] = mm(left[0], lop[m, 0])
        freq[m, 1] = mm(left[1], lop[m, 1])

    def backward(m, modify, consume):
        for parity in range(2):
            for q in range(HALF // CHUNK):
                top = pl.ds(q * CHUNK, CHUNK)
                bot = pl.ds(HALF + q * CHUNK, CHUNK)
                table_rows = pl.ds(parity * HALF + q * CHUNK, CHUNK)
                re, im = modify(table_rows, freq[m, parity, top, :], freq[m, parity, bot, :])
                put_left(m, parity, q * CHUNK, re)
                put_left(m, parity, HALF + q * CHUNK, im)
        tmp[m, 0] = mm(left[2], lop[m, 0])
        tmp[m, 1] = mm(left[3], lop[m, 1])
        for q in range(HALF // CHUNK):
            top = pl.ds(q * CHUNK, CHUNK)
            bot = pl.ds(HALF + q * CHUNK, CHUNK)
            gr, gi = tmp[m, 0, top, :], tmp[m, 0, bot, :]
            hr, hi = tmp[m, 1, top, :], tmp[m, 1, bot, :]
            for rows, re, im in ((top, gr + hr, gi + hi), (bot, gr - hr, gi - hi)):
                put_right(m, 0, rows, jnp.concatenate([re[:, :HALF], im[:, :HALF]], axis=1))
                put_right(m, 1, rows, jnp.concatenate([re[:, HALF:], im[:, HALF:]], axis=1))
        tmp[m, 0] = mm(rop[m, 0], right[0])
        tmp[m, 1] = mm(rop[m, 1], right[1])
        for q in range(FRAME // CHUNK):
            rows = pl.ds(q * CHUNK, CHUNK)
            g, h = tmp[m, 0, rows, :], tmp[m, 1, rows, :]
            re = jnp.concatenate([g[:, :HALF] + h[:, :HALF], g[:, :HALF] - h[:, :HALF]], axis=1)
            im = jnp.concatenate([g[:, HALF:] + h[:, HALF:], g[:, HALF:] - h[:, HALF:]], axis=1)
            consume(m, rows, re, im)

    def times(a_re, a_im, b_re, b_im):
        return a_re * b_re - a_im * b_im, a_re * b_im + a_im * b_re

    def conj_times(a_re, a_im, b_re, b_im):
        return a_re * b_re + a_im * b_im, a_re * b_im - a_im * b_re

    def pair(ref, *at):
        return ref[(*at[:-1], 0, at[-1], slice(None))], ref[(*at[:-1], 1, at[-1], slice(None))]

    def modes(step):
        for m in range(MODES):
            step(m)

    def through_first_slice(f):
        def keep(m, rows, re, im):
            u1[f, m, 0, rows, :] = re
            u1[f, m, 1, rows, :] = im

        modes(lambda m: forward(m, lambda m, rows: times(*pair(probe, m, rows), *pair(obj, f, 0, rows))))
        modes(lambda m: backward(m, lambda rows, re, im: times(kern[0, rows, :], kern[1, rows, :], re, im), keep))

    def keep_wave(f):
        def keep(m, rows, re, im):
            wave[f, m, 0, rows, :] = re
            wave[f, m, 1, rows, :] = im
        return keep

    def terms(f, incoming):
        _, row_shift, _, col_shift = corner(pos_ref, f)
        for q in range(FRAME // CHUNK):
            rows = pl.ds(q * CHUNK, CHUNK)
            total = None
            for m in range(MODES):
                one = conj_times(*incoming(m, rows), *pair(wave, f, m, rows))
                total = one if total is None else (total[0] + one[0], total[1] + one[1])
            for c in range(2):
                padded[c, pl.ds(8 + q * CHUNK, CHUNK), :] = total[c]
        beside = jnp.zeros((TALL, HALF), F32)
        for c in range(2):
            for q in range(264 // TALL):
                x = pltpu.roll(padded[c, pl.ds(q * TALL, TALL + 8), :], lax.rem(TALL + row_shift, TALL + 8), 0)[:TALL]
                x = pltpu.roll(jnp.concatenate([x, beside], axis=1), col_shift, 1)
                for j in range(3):
                    placed[f, c, j, pl.ds(BLANK_ROWS // 8 + q * TALL // 8, TALL // 8)] = x[:, j * HALF:(j + 1) * HALF].reshape(TALL // 8, 8, HALF)

    def collect(s):
        corners = [corner(pos_ref, f) for f in range(2)]

        @pl.loop(0, STRIPS)
        def _(i):
            spots = []
            for block, _, cs, _ in corners:
                j = i - cs
                inside = jnp.logical_and(j >= 0, j < 3)
                spots.append((jnp.where(inside, j, 3), BLANK_ROWS // 8 - block))
            for c in range(2):
                for n in range(ROWS_EXT // 8):
                    x, y = [placed[f, c, j, row + n] for f, (j, row) in enumerate(spots)]
                    gs[s][i, c, pl.ds(n * 8, 8), :] = x + y

    g_out_src, g_sib_src = aligned(384 * me.core), aligned(384 * (1 - me.core))
    g_out_rows, g_sib_rows = aligned(HALO + HALO * me.core), aligned(HALO + HALO * (1 - me.core))

    def strip(half, k):
        return half * 4 + (me.x + k) % 4

    edges, relays, crossing, last = {}, {}, {}, {}

    def start_edges(s, k):
        for h in range(2):
            i = strip(h, k)
            edges[s, k, h, 0] = send.copy(gs[s].at[i, :, pl.ds(g_out_src, HALO), :], edge_out.at[s, k, h], outer)
            edges[s, k, h, 1] = send.copy(gs[s].at[i, :, pl.ds(g_sib_src, HALO), :], edge_sib.at[s, k, h], sibling)

    def take_edges(s, k):
        g = gs[s]
        for h in range(2):
            edges[s, k, h, 0].wait_recv()
            edges[s, k, h, 1].wait_recv()
            i = strip(h, k)
            g[i, :, pl.ds(g_out_rows, HALO), :] += edge_out[s, k, h]
            g[i, :, pl.ds(g_sib_rows, HALO), :] += edge_sib[s, k, h]
        for h in range(2):
            i = strip(h, k)
            if k == 2:
                relays[s, h, 0] = send.copy(g.at[i, 0, mine, :], rb.at[s, h, 0], ahead)
                relays[s, h, 1] = send.copy(g.at[i, 1, mine, :], rb.at[s, h, 1], behind)
            if k == 1:
                crossing[s, h, 0, 1] = send.copy(g.at[i, 1, mine, :], xb.at[s, h, 0, 1], ahead)
            if k == 3:
                crossing[s, h, 1, 0] = send.copy(g.at[i, 0, mine, :], xb.at[s, h, 1, 0], behind)

    def take_relays(s):
        for h in range(2):
            for way, k, peer in ((0, 1, ahead), (1, 3, behind)):
                relays[s, h, way].wait_recv()
                i = strip(h, k)
                gs[s][i, way, mine, :] += rb[s, h, way]
                crossing[s, h, way, way] = send.copy(gs[s].at[i, way, mine, :], xb.at[s, h, way, way], peer)

    def fold(s):
        for h in range(2):
            for way in range(2):
                for c in range(2):
                    crossing[s, h, way, c].wait_recv()
            part[s, h] = gs[s][strip(h, 0), :, mine, :] + xb[s, h, 0] + xb[s, h, 1]
        last[s] = send.copy(part.at[s, 1 - me.zh], zb.at[s], z_peer)

    for s in range(SLICES):
        own_to_z(s)
        own_to_x(s)
    for s in range(SLICES):
        pass_edges(f_own, s, own_ref)
    for load in loads[:4]:
        load.wait()
    perm, perm_t = perms[0], perms[1]
    bg[...] = reorder_exact(back_raw[...], perm, perm_t)
    phase = reorder_exact(phase_raw[...], perm, perm_t)
    kern[0] = jnp.cos(phase)
    kern[1] = jnp.sin(phase)
    from_z(0)
    from_x(own_half, 0)
    from_z(1)
    from_x(own_half, 1)
    for f in range(2):
        half = mm(perm, counts_raw[f].astype(F32).astype(BF16)).astype(BF16)
        cnt[f] = mm(half, perm_t)
    from_x(other_half, 0)
    placed[...] = jnp.zeros_like(placed)
    padded[...] = jnp.zeros_like(padded)
    from_relay(own_half, 0)
    from_relay(other_half, 0)
    for load in loads[4:]:
        load.wait()
    from_relay(own_half, 1)
    cut(0)
    from_x(other_half, 1)
    through_first_slice(0)
    from_relay(other_half, 1)
    through_first_slice(1)
    cut(1)

    @pl.loop(0, 2)
    def _(f):
        modes(lambda m: forward(m, lambda m, rows: times(*pair(u1, f, m, rows), *pair(obj, f, 1, rows))))
        for parity in range(2):
            for q in range(HALF // CHUNK):
                top = pl.ds(q * CHUNK, CHUNK)
                bot = pl.ds(HALF + q * CHUNK, CHUNK)
                rows = pl.ds(parity * HALF + q * CHUNK, CHUNK)
                level = bg[rows, :]
                for m in range(MODES):
                    re, im = freq[m, parity, top, :], freq[m, parity, bot, :]
                    level = level + re * re + im * im
                cnt[f, rows, :] = 1.0 - cnt[f, rows, :] / level
        modes(lambda m: backward(m, lambda rows, re, im: (re * cnt[f, rows, :], im * cnt[f, rows, :]), keep_wave(f)))
        terms(f, lambda m, rows: pair(u1, f, m, rows))

    collect(1)
    for k in (2, 1, 3):
        start_edges(1, k)

    for f in range(2):
        modes(lambda m: forward(m, lambda m, rows: conj_times(*pair(obj, f, 1, rows), *pair(wave, f, m, rows))))
        if f == 0:
            take_edges(1, 2)
        modes(lambda m: backward(m, lambda rows, re, im: conj_times(kern[0, rows, :], kern[1, rows, :], re, im), keep_wave(f)))
        if f == 0:
            take_edges(1, 1)
            take_edges(1, 3)
            start_edges(1, 0)
        terms(f, lambda m, rows: pair(probe, m, rows))
        for m in range(MODES):
            for q in range(FRAME // CHUNK):
                rows = pl.ds(q * CHUNK, CHUNK)
                re, im = conj_times(*pair(obj, f, 0, rows), *pair(wave, f, m, rows))
                if f == 0:
                    p_sum[m, 0, rows, :] = re
                    p_sum[m, 1, rows, :] = im
                else:
                    p_sum[m, 0, rows, :] += re
                    p_sum[m, 1, rows, :] += im
        if f == 0:
            take_relays(1)

    collect(0)
    for k in (2, 1, 3):
        start_edges(0, k)
    other = send.copy(p_sum.at[1 - me.core], sb, sibling)
    take_edges(1, 0)
    start_edges(0, 0)

    quarter = lambda y: pl.ds(aligned(64 * y), 64)
    spot = lambda q: (q // 8, pl.ds(aligned(8 * (q % 8)), 8))
    other.wait_recv()
    ph[...] = p_sum[me.core] + sb[...]
    y_sums = [send.copy(ph.at[:, quarter((me.y + k) % 4), :], yb.at[k - 1], upward[k - 1]) for k in (1, 2, 3)]
    take_edges(0, 2)
    take_edges(0, 1)
    take_edges(0, 3)
    for made in y_sums:
        made.wait_recv()
    pq[...] = ph[:, quarter(me.y), :] + yb[0] + yb[1] + yb[2]
    plane_sums = []
    for j, (q, peer) in enumerate(plane):
        c, rows = spot(q)
        plane_sums.append(send.copy(pq.at[c, rows, :], xzb.at[j], peer))
    fold(1)
    take_relays(0)
    for made in plane_sums:
        made.wait_recv()
    q = me.z * 4 + me.x
    c, rows = spot(q)
    total = pq[c, rows, :]
    for j in range(15):
        total = total + xzb[j]
    final_rows = pl.ds(aligned(64 * me.y + 8 * (q % 8)), 8)
    pout_ref[me.core, c, final_rows, :] = total
    spread = pout_ref.at[me.core, c, final_rows, :]
    plane_gather = [send.copy(spread, spread, peer) for _, peer in plane]
    take_edges(0, 0)
    last[1].wait_recv()
    out_ref[1] = part[1, me.zh] + zb[1]
    for made in plane_gather:
        made.wait_recv()
    spread_y = pout_ref.at[me.core, :, quarter(me.y), :]
    y_gather = [send.copy(spread_y, spread_y, peer) for peer in upward]
    for made in y_gather:
        made.wait_recv()
    final = send.copy(pout_ref.at[me.core], pout_ref.at[me.core], sibling)
    fold(0)
    last[0].wait_recv()
    out_ref[0] = part[0, me.zh] + zb[0]
    final.wait_recv()
    send.finish()


def shards(object_slices, probe_modes, prop_phase, background, positions, counts):
    lefts, rights, perm_pair = dft_constants()
    vmem = pl.BlockSpec(memory_space=pltpu.VMEM)
    square = (FRAME, FRAME)
    half_strip = (2, HALO, HALF)
    full_strip = (2, FRAME, HALF)
    tile = (STRIPS, 2, ROWS_EXT, HALF)
    blocks = (STRIPS, 2, ROWS_EXT // 8, 8, HALF)
    own = object_slices.reshape(SLICES, 2, FRAME // 8, 8, HALF)
    return pl.pallas_call(
        gradient_kernel,
        out_shape=(
            jax.ShapeDtypeStruct((SLICES,) + full_strip, F32),
            jax.ShapeDtypeStruct((MODES, 2) + square, F32),
        ),
        in_specs=[pl.BlockSpec(memory_space=pltpu.SMEM)] + [pl.BlockSpec(memory_space=pl.ANY)] * 8,
        out_specs=(vmem, vmem),
        scratch_shapes=[
            pltpu.VMEM(blocks, F32),
            pltpu.VMEM(blocks, F32),
            pltpu.VMEM(tile, F32),
            pltpu.VMEM(tile, F32),
            pltpu.VMEM((MODES, 2) + square, F32),
            pltpu.VMEM(square, F32),
            pltpu.VMEM(square, F32),
            pltpu.VMEM((2,) + square, jnp.int32),
            pltpu.VMEM((4, FRAME, 3 * FRAME), BF16),
            pltpu.VMEM((4, 3 * FRAME, FRAME), BF16),
            pltpu.VMEM((2,) + square, BF16),
            pltpu.VMEM((2, SLICES, 2) + square, F32),
            pltpu.VMEM((2,) + square, F32),
            pltpu.VMEM(square, F32),
            pltpu.VMEM((2,) + square, F32),
            pltpu.VMEM((2, MODES, 2) + square, F32),
            pltpu.VMEM((2, MODES, 2) + square, F32),
            pltpu.VMEM((MODES, 2, FRAME, 3 * FRAME), BF16),
            pltpu.VMEM((MODES, 2, 3 * FRAME, FRAME), BF16),
            pltpu.VMEM((MODES, 2) + square, F32),
            pltpu.VMEM((MODES, 2) + square, F32),
            pltpu.VMEM((2, FRAME + 16, FRAME), F32),
            pltpu.VMEM((2, 2, 4, PAD_ROWS // 8, 8, HALF), F32),
            pltpu.VMEM((2, 4, 2) + half_strip, F32),
            pltpu.VMEM((2, 4, 2) + half_strip, F32),
            pltpu.VMEM((2, 2, 2, FRAME, HALF), F32),
            pltpu.VMEM((2, 2, 2) + full_strip, F32),
            pltpu.VMEM((2, 2) + full_strip, F32),
            pltpu.VMEM((2,) + full_strip, F32),
            pltpu.VMEM((MODES, 2) + square, F32),
            pltpu.VMEM((2,) + square, F32),
            pltpu.VMEM((2,) + square, F32),
            pltpu.VMEM((3, 2, 64, FRAME), F32),
            pltpu.VMEM((2, 64, FRAME), F32),
            pltpu.VMEM((15, 8, FRAME), F32),
            pltpu.SemaphoreType.DMA((9,)),
            pltpu.SemaphoreType.DMA((COPIES,)),
            pltpu.SemaphoreType.DMA((COPIES,)),
        ],
        compiler_params=pltpu.CompilerParams(collective_id=1, has_side_effects=True, vmem_limit_bytes=60 << 20),
        name="gradient",
    )(positions, own, probe_modes, prop_phase, background, counts,
      jnp.asarray(lefts), jnp.asarray(rights), jnp.asarray(perm_pair))


def solution(mesh):
    in_specs = (
        P(None, None, "tile", "frame"),
        P(),
        P(),
        P(),
        P(("tile", "frame"), None),
        P(("tile", "frame"), None, None),
    )
    out_specs = (P(None, None, "tile", "frame"), P())
    return jax.shard_map(shards, mesh=mesh, in_specs=in_specs, out_specs=out_specs, check_vma=False)
```

```python
import numpy as np
import ml_dtypes
import jax
import jax.numpy as jnp
from jax import lax
from jax.experimental import pallas as pl
from jax.experimental.pallas import tpu as pltpu
from jax.sharding import PartitionSpec as P

FRAME = 256
HALF = 128
SLICES = 2
MODES = 2
HALO = 128
ROWS_EXT = 512
STRIPS = 8
WIN_COLS = 384
CHUNK = 32
TALL = 88
BLANK_ROWS = 248
PAD_ROWS = 2 * BLANK_ROWS + 264
F32 = jnp.float32
BF16 = jnp.bfloat16


def dft_constants():
    k = np.arange(HALF)[:, None]
    n = np.arange(HALF)[None, :]
    mats = []
    for odd in (0, 1):
        turns = ((2 * k + odd) * n) % FRAME
        angle = -2.0 * np.pi * turns / FRAME
        c, s = np.cos(angle) / 16.0, np.sin(angle) / 16.0
        mats.append(np.block([[c, -s], [s, c]]))
    even, odd = mats
    lefts, rights = [], []
    for m in (even, odd, even.T, odd.T):
        hi = m.astype(ml_dtypes.bfloat16)
        lo = (m - hi.astype(np.float64)).astype(ml_dtypes.bfloat16)
        lefts.append(np.concatenate([hi, hi, lo], axis=1))
        rights.append(np.concatenate([hi, hi, lo], axis=0))
    perm = np.zeros((FRAME, FRAME))
    order = np.concatenate([np.arange(0, FRAME, 2), np.arange(1, FRAME, 2)])
    perm[np.arange(FRAME), order] = 1.0
    perms = np.stack([perm, perm.T]).astype(ml_dtypes.bfloat16)
    return np.stack(lefts), np.stack(rights), perms


def mm(a, b):
    return jnp.dot(a, b, preferred_element_type=F32)


def parts3(x):
    a = x.astype(BF16)
    r = x - a.astype(F32)
    b = r.astype(BF16)
    c = (r - b.astype(F32)).astype(BF16)
    return a, b, c


def reorder_exact(x, perm, perm_t):
    a, b, c = parts3(x)
    y = mm(perm, a) + mm(perm, b) + mm(perm, c)
    a, b, c = parts3(y)
    return mm(a, perm_t) + mm(b, perm_t) + mm(c, perm_t)


def corner(pos_ref, f):
    r, c = pos_ref[f, 0], pos_ref[f, 1]
    block = jnp.minimum(r // 8, 31)
    cs = jnp.minimum(c // HALF, 5)
    return block, r - block * 8, cs, c - cs * HALF


MESH = pl.DeviceIdType.MESH


class Place:
    def __init__(self):
        tile, frame = lax.axis_index("tile"), lax.axis_index("frame")
        self.y, self.zl, self.core = tile // 4, (tile // 2) % 2, tile % 2
        self.zh, self.x = frame // 4, frame % 4
        self.z = self.zh * 2 + self.zl

    def at(self, y=None, zl=None, core=None, zh=None, x=None):
        pick = lambda given, own: own if given is None else given
        tile = (pick(y, self.y) * 2 + pick(zl, self.zl)) * 2 + pick(core, self.core)
        return tile, pick(zh, self.zh) * 4 + pick(x, self.x)

    def along_x(self, k):
        return self.at(x=(self.x + k) % 4)

    def along_y(self, k):
        return self.at(y=(self.y + k) % 4)

    def in_plane(self, j):
        q = (self.z * 4 + self.x + j) % 16
        z = q // 4
        return q, self.at(zl=z % 2, zh=z // 2, x=q % 4)

    def z_peer(self):
        return self.at(zh=1 - self.zh)

    def sibling(self):
        return self.at(core=1 - self.core)

    def outer(self):
        turn = self.core * self.zl + (1 - self.core) * (1 - self.zl)
        step = turn * (2 * self.core - 1)
        zh = turn * (1 - self.zh) + (1 - turn) * self.zh
        return self.at(y=(self.y + step + 4) % 4, zl=1 - self.zl, core=1 - self.core, zh=zh)


def greet(peers):
    barrier = pltpu.get_barrier_semaphore()
    for peer in peers:
        pl.semaphore_signal(barrier, inc=1, device_id=peer, device_id_type=MESH)
    pl.semaphore_wait(barrier, len(peers))


class Sender:
    def __init__(self, send_sems, recv_sems):
        self.send_sems, self.recv_sems = send_sems, recv_sems
        self.started = []

    def copy(self, src, dst, peer):
        n = len(self.started)
        made = pltpu.make_async_remote_copy(
            src_ref=src, dst_ref=dst, send_sem=self.send_sems.at[n], recv_sem=self.recv_sems.at[n],
            device_id=peer, device_id_type=MESH,
        )
        made.start()
        self.started.append(made)
        return made

    def finish(self):
        for made in self.started:
            made.wait_send()


def aligned(row):
    return pl.multiple_of(row, 8)


GATHER_COPIES = 6 + 4 + 8 + 16 + 4
SCATTER_COPIES = 32 + 8 + 16 + 2 + 1 + 3 + 15 + 15 + 3 + 1
COPIES = GATHER_COPIES + SCATTER_COPIES


def gradient_kernel(
    pos_ref, own_ref, probe_in, phase_in, back_in, counts_in, left_in, right_in, perm_in,
    out_ref, pout_ref,
    ext_0, ext_1, g_0, g_1, probe, phase_raw, back_raw, counts_raw, left, right, perms,
    obj, kern, bg, cnt, wave, u1, rop, lop, tmp, freq, padded, placed,
    edge_out, edge_sib, rb, xb, part, zb, p_sum, sb, ph, yb, pq, xzb,
    local_sems, send_sems, recv_sems,
):
    exts, gs = (ext_0, ext_1), (g_0, g_1)
    me = Place()
    f_own, f_other = me.zh * 4 + me.x, (1 - me.zh) * 4 + me.x
    sibling, outer, z_peer = me.sibling(), me.outer(), me.z_peer()
    ahead, behind = me.along_x(1), me.along_x(3)
    upward = [me.along_y(k) for k in (1, 2, 3)]
    plane = [me.in_plane(j) for j in range(1, 16)]

    loads = [
        pltpu.make_async_copy(src, dst, local_sems.at[n])
        for n, (src, dst) in enumerate((
            (perm_in, perms), (back_in, back_raw), (phase_in, phase_raw), (counts_in, counts_raw),
            (probe_in, probe), (left_in, left), (right_in, right),
        ))
    ]
    for load in loads:
        load.start()
    mine, own_blocks = pl.ds(HALO, FRAME), pl.ds(16, 32)
    keeps = [
        pltpu.make_async_copy(own_ref.at[s], exts[s].at[f_own, :, own_blocks], local_sems.at[len(loads) + s])
        for s in range(SLICES)
    ]
    for keep in keeps:
        keep.start()

    greet([sibling, outer] + upward + [peer for _, peer in plane])
    send = Sender(send_sems, recv_sems)

    out_src, out_dst = 16 + 16 * me.core, 48 * (1 - me.core)
    sib_src, sib_dst = 16 + 16 * (1 - me.core), 48 * me.core
    margins = ([], [])

    def pass_edges(strip, s, ref=None):
        base = exts[s].at[strip] if ref is None else ref.at[s]
        shift = 0 if ref is None else 16
        margins[s].append(send.copy(
            base.at[:, pl.ds(out_src - shift, 16)], exts[s].at[strip, :, pl.ds(out_dst, 16)], outer
        ))

    def pass_half(which, s):
        group = exts[s].at[pl.ds(half_of[which] * 4, 4)]
        margins[s].append(send.copy(
            group.at[:, :, pl.ds(sib_src, 16)], group.at[:, :, pl.ds(sib_dst, 16)], sibling
        ))

    to_z, to_x, relayed = {}, {}, {}
    own_half, other_half = 0, 1
    half_of = (me.zh, 1 - me.zh)

    def strip_at(which, k):
        return half_of[which] * 4 + (me.x + k + 4) % 4

    def own_to_z(s):
        to_z[s] = send.copy(own_ref.at[s], exts[s].at[f_own, :, own_blocks], z_peer)

    def own_to_x(s):
        to_x[own_half, s, 0] = send.copy(own_ref.at[s], exts[s].at[f_own, :, own_blocks], ahead)
        to_x[own_half, s, 1] = send.copy(own_ref.at[s], exts[s].at[f_own, :, own_blocks], behind)

    def from_z(s):
        to_z[s].wait_recv()
        whole = exts[s].at[f_other, :, own_blocks]
        to_x[other_half, s, 0] = send.copy(whole, whole, ahead)
        to_x[other_half, s, 1] = send.copy(whole, whole, behind)
        pass_edges(f_other, s)

    def from_x(which, s):
        for way, peer, k in ((0, ahead, -1), (1, behind, 1)):
            to_x[which, s, way].wait_recv()
            half = exts[s].at[strip_at(which, k), way, own_blocks]
            relayed[which, s, way] = send.copy(half, half, peer)
        for k in (-1, 1):
            pass_edges(strip_at(which, k), s)

    def from_relay(which, s):
        if which == own_half:
            keeps[s].wait()
        for way in range(2):
            relayed[which, s, way].wait_recv()
        pass_edges(strip_at(which, 2), s)
        pass_half(which, s)

    def cut(s):
        for made in margins[s]:
            made.wait_recv()

        @pl.loop(0, 2)
        def _(f):
            block, row_shift, cs, col_shift = corner(pos_ref, f)
            for p in range(2):
                for q in range(FRAME // CHUNK):
                    x = jnp.concatenate([
                        jnp.concatenate([exts[s][cs + j, p, block + q * CHUNK // 8 + n] for n in range(CHUNK // 8 + 1)], axis=0)
                        for j in range(3)
                    ], axis=1)
                    x = pltpu.roll(x, lax.rem(WIN_COLS - col_shift, WIN_COLS), 1)[:, :FRAME]
                    x = pltpu.roll(x, lax.rem(CHUNK + 8 - row_shift, CHUNK + 8), 0)
                    obj[f, s, p, pl.ds(q * CHUNK, CHUNK), :] = x[:CHUNK]

    def put_right(m, parity, rows, x):
        hi = x.astype(BF16)
        lo = (x - hi.astype(F32)).astype(BF16)
        rop[m, parity, rows, 0:256] = hi
        rop[m, parity, rows, 256:512] = lo
        rop[m, parity, rows, 512:768] = hi

    def put_left(m, parity, start, x):
        hi = x.astype(BF16)
        lo = (x - hi.astype(F32)).astype(BF16)
        n = x.shape[0]
        lop[m, parity, pl.ds(start, n), :] = hi
        lop[m, parity, pl.ds(256 + start, n), :] = lo
        lop[m, parity, pl.ds(512 + start, n), :] = hi

    def forward(m, produce):
        for q in range(FRAME // CHUNK):
            rows = pl.ds(q * CHUNK, CHUNK)
            re, im = produce(m, rows)
            a, b = re[:, :HALF], re[:, HALF:]
            c, d = im[:, :HALF], im[:, HALF:]
            put_right(m, 0, rows, jnp.concatenate([a + b, c + d], axis=1))
            put_right(m, 1, rows, jnp.concatenate([a - b, c - d], axis=1))
        tmp[m, 0] = mm(rop[m, 0], right[2])
        tmp[m, 1] = mm(rop[m, 1], right[3])
        for q in range(HALF // CHUNK):
            top = pl.ds(q * CHUNK, CHUNK)
            bot = pl.ds(HALF + q * CHUNK, CHUNK)
            et, eb = tmp[m, 0, top, :], tmp[m, 0, bot, :]
            ot, ob = tmp[m, 1, top, :], tmp[m, 1, bot, :]
            for parity, e, o in ((0, et + eb, ot + ob), (1, et - eb, ot - ob)):
                put_left(m, parity, q * CHUNK, jnp.concatenate([e[:, :HALF], o[:, :HALF]], axis=1))
                put_left(m, parity, HALF + q * CHUNK, jnp.concatenate([e[:, HALF:], o[:, HALF:]], axis=1))
        freq[m, 0] = mm(left[0], lop[m, 0])
        freq[m, 1] = mm(left[1], lop[m, 1])

    def backward(m, modify, consume):
        for parity in range(2):
            for q in range(HALF // CHUNK):
                top = pl.ds(q * CHUNK, CHUNK)
                bot = pl.ds(HALF + q * CHUNK, CHUNK)
                table_rows = pl.ds(parity * HALF + q * CHUNK, CHUNK)
                re, im = modify(table_rows, freq[m, parity, top, :], freq[m, parity, bot, :])
                put_left(m, parity, q * CHUNK, re)
                put_left(m, parity, HALF + q * CHUNK, im)
        tmp[m, 0] = mm(left[2], lop[m, 0])
        tmp[m, 1] = mm(left[3], lop[m, 1])
        for q in range(HALF // CHUNK):
            top = pl.ds(q * CHUNK, CHUNK)
            bot = pl.ds(HALF + q * CHUNK, CHUNK)
            gr, gi = tmp[m, 0, top, :], tmp[m, 0, bot, :]
            hr, hi = tmp[m, 1, top, :], tmp[m, 1, bot, :]
            for rows, re, im in ((top, gr + hr, gi + hi), (bot, gr - hr, gi - hi)):
                put_right(m, 0, rows, jnp.concatenate([re[:, :HALF], im[:, :HALF]], axis=1))
                put_right(m, 1, rows, jnp.concatenate([re[:, HALF:], im[:, HALF:]], axis=1))
        tmp[m, 0] = mm(rop[m, 0], right[0])
        tmp[m, 1] = mm(rop[m, 1], right[1])
        for q in range(FRAME // CHUNK):
            rows = pl.ds(q * CHUNK, CHUNK)
            g, h = tmp[m, 0, rows, :], tmp[m, 1, rows, :]
            re = jnp.concatenate([g[:, :HALF] + h[:, :HALF], g[:, :HALF] - h[:, :HALF]], axis=1)
            im = jnp.concatenate([g[:, HALF:] + h[:, HALF:], g[:, HALF:] - h[:, HALF:]], axis=1)
            consume(m, rows, re, im)

    def times(a_re, a_im, b_re, b_im):
        return a_re * b_re - a_im * b_im, a_re * b_im + a_im * b_re

    def conj_times(a_re, a_im, b_re, b_im):
        return a_re * b_re + a_im * b_im, a_re * b_im - a_im * b_re

    def pair(ref, *at):
        return ref[(*at[:-1], 0, at[-1], slice(None))], ref[(*at[:-1], 1, at[-1], slice(None))]

    def modes(step):
        for m in range(MODES):
            step(m)

    def through_first_slice(f):
        def keep(m, rows, re, im):
            u1[f, m, 0, rows, :] = re
            u1[f, m, 1, rows, :] = im

        modes(lambda m: forward(m, lambda m, rows: times(*pair(probe, m, rows), *pair(obj, f, 0, rows))))
        modes(lambda m: backward(m, lambda rows, re, im: times(kern[0, rows, :], kern[1, rows, :], re, im), keep))

    def keep_wave(f):
        def keep(m, rows, re, im):
            wave[f, m, 0, rows, :] = re
            wave[f, m, 1, rows, :] = im
        return keep

    def terms(f, incoming):
        _, row_shift, _, col_shift = corner(pos_ref, f)
        for q in range(FRAME // CHUNK):
            rows = pl.ds(q * CHUNK, CHUNK)
            total = None
            for m in range(MODES):
                one = conj_times(*incoming(m, rows), *pair(wave, f, m, rows))
                total = one if total is None else (total[0] + one[0], total[1] + one[1])
            for c in range(2):
                padded[c, pl.ds(8 + q * CHUNK, CHUNK), :] = total[c]
        beside = jnp.zeros((TALL, HALF), F32)
        for c in range(2):
            for q in range(264 // TALL):
                x = pltpu.roll(padded[c, pl.ds(q * TALL, TALL + 8), :], lax.rem(TALL + row_shift, TALL + 8), 0)[:TALL]
                x = pltpu.roll(jnp.concatenate([x, beside], axis=1), col_shift, 1)
                for j in range(3):
                    placed[f, c, j, pl.ds(BLANK_ROWS // 8 + q * TALL // 8, TALL // 8)] = x[:, j * HALF:(j + 1) * HALF].reshape(TALL // 8, 8, HALF)

    def collect(s):
        corners = [corner(pos_ref, f) for f in range(2)]

        @pl.loop(0, STRIPS)
        def _(i):
            spots = []
            for block, _, cs, _ in corners:
                j = i - cs
                inside = jnp.logical_and(j >= 0, j < 3)
                spots.append((jnp.where(inside, j, 3), BLANK_ROWS // 8 - block))
            for c in range(2):
                for n in range(ROWS_EXT // 8):
                    x, y = [placed[f, c, j, row + n] for f, (j, row) in enumerate(spots)]
                    gs[s][i, c, pl.ds(n * 8, 8), :] = x + y

    g_out_src, g_sib_src = aligned(384 * me.core), aligned(384 * (1 - me.core))
    g_out_rows, g_sib_rows = aligned(HALO + HALO * me.core), aligned(HALO + HALO * (1 - me.core))

    def strip(half, k):
        return half * 4 + (me.x + k) % 4

    edges, relays, crossing, last = {}, {}, {}, {}
    half_order = (1 - me.zh, me.zh)

    def start_edges(s, k):
        for h in range(2):
            i = strip(h, k)
            edges[s, k, h, 0] = send.copy(gs[s].at[i, :, pl.ds(g_out_src, HALO), :], edge_out.at[s, k, h], outer)
            edges[s, k, h, 1] = send.copy(gs[s].at[i, :, pl.ds(g_sib_src, HALO), :], edge_sib.at[s, k, h], sibling)

    def take_edges(s, k):
        g = gs[s]
        for h in range(2):
            edges[s, k, h, 0].wait_recv()
            edges[s, k, h, 1].wait_recv()
            i = strip(h, k)
            g[i, :, pl.ds(g_out_rows, HALO), :] += edge_out[s, k, h]
            g[i, :, pl.ds(g_sib_rows, HALO), :] += edge_sib[s, k, h]
        for n, h in enumerate(half_order):
            i = strip(h, k)
            if k == 2:
                relays[s, n, 0] = send.copy(g.at[i, 0, mine, :], rb.at[s, n, 0], ahead)
                relays[s, n, 1] = send.copy(g.at[i, 1, mine, :], rb.at[s, n, 1], behind)
            if k == 1:
                crossing[s, n, 0, 1] = send.copy(g.at[i, 1, mine, :], xb.at[s, n, 0, 1], ahead)
            if k == 3:
                crossing[s, n, 1, 0] = send.copy(g.at[i, 0, mine, :], xb.at[s, n, 1, 0], behind)

    def take_relays(s):
        for n, h in enumerate(half_order):
            for way, k, peer in ((0, 1, ahead), (1, 3, behind)):
                relays[s, n, way].wait_recv()
                i = strip(h, k)
                gs[s][i, way, mine, :] += rb[s, n, way]
                crossing[s, n, way, way] = send.copy(gs[s].at[i, way, mine, :], xb.at[s, n, way, way], peer)

    def take_crossing(s, n):
        for way in range(2):
            for c in range(2):
                crossing[s, n, way, c].wait_recv()
        return gs[s][strip(half_order[n], 0), :, mine, :] + xb[s, n, 0] + xb[s, n, 1]

    def fold(s):
        part[s] = take_crossing(s, 0)
        last[s] = send.copy(part.at[s], zb.at[s], z_peer)

    def finish(s):
        own_sum = take_crossing(s, 1)
        last[s].wait_recv()
        out_ref[s] = own_sum + zb[s]

    own_to_z(0)
    own_to_x(0)
    own_to_z(1)
    own_to_x(1)
    pass_edges(f_own, 0, own_ref)
    for load in loads[:4]:
        load.wait()
    perm, perm_t = perms[0], perms[1]
    bg[...] = reorder_exact(back_raw[...], perm, perm_t)
    phase = reorder_exact(phase_raw[...], perm, perm_t)
    from_z(0)
    from_x(own_half, 0)
    kern[0] = jnp.cos(phase)
    kern[1] = jnp.sin(phase)
    from_z(1)
    for f in range(2):
        half = mm(perm, counts_raw[f].astype(F32).astype(BF16)).astype(BF16)
        cnt[f] = mm(half, perm_t)
    from_x(own_half, 1)
    padded[...] = jnp.zeros_like(padded)
    placed[...] = jnp.zeros_like(placed)
    from_x(other_half, 0)
    from_relay(own_half, 0)
    from_relay(other_half, 0)
    pass_edges(f_own, 1, own_ref)
    for load in loads[4:]:
        load.wait()
    from_x(other_half, 1)
    from_relay(own_half, 1)
    cut(0)
    through_first_slice(0)
    from_relay(other_half, 1)
    through_first_slice(1)
    cut(1)

    @pl.loop(0, 2)
    def _(f):
        modes(lambda m: forward(m, lambda m, rows: times(*pair(u1, f, m, rows), *pair(obj, f, 1, rows))))
        for parity in range(2):
            for q in range(HALF // CHUNK):
                top = pl.ds(q * CHUNK, CHUNK)
                bot = pl.ds(HALF + q * CHUNK, CHUNK)
                rows = pl.ds(parity * HALF + q * CHUNK, CHUNK)
                level = bg[rows, :]
                for m in range(MODES):
                    re, im = freq[m, parity, top, :], freq[m, parity, bot, :]
                    level = level + re * re + im * im
                cnt[f, rows, :] = 1.0 - cnt[f, rows, :] / level
        modes(lambda m: backward(m, lambda rows, re, im: (re * cnt[f, rows, :], im * cnt[f, rows, :]), keep_wave(f)))
        terms(f, lambda m, rows: pair(u1, f, m, rows))

    collect(1)
    for k in (2, 1, 3, 0):
        start_edges(1, k)

    for f in range(2):
        modes(lambda m: forward(m, lambda m, rows: conj_times(*pair(obj, f, 1, rows), *pair(wave, f, m, rows))))
        if f == 0:
            take_edges(1, 2)
        else:
            take_relays(1)
        modes(lambda m: backward(m, lambda rows, re, im: conj_times(kern[0, rows, :], kern[1, rows, :], re, im), keep_wave(f)))
        if f == 0:
            take_edges(1, 1)
            take_edges(1, 3)
        terms(f, lambda m, rows: pair(probe, m, rows))
        for m in range(MODES):
            for q in range(FRAME // CHUNK):
                rows = pl.ds(q * CHUNK, CHUNK)
                re, im = conj_times(*pair(obj, f, 0, rows), *pair(wave, f, m, rows))
                if f == 0:
                    p_sum[m, 0, rows, :] = re
                    p_sum[m, 1, rows, :] = im
                else:
                    p_sum[m, 0, rows, :] += re
                    p_sum[m, 1, rows, :] += im

    other = send.copy(p_sum.at[1 - me.core], sb, sibling)
    collect(0)
    for k in (2, 1, 3):
        start_edges(0, k)
    quarter = lambda y: pl.ds(aligned(64 * y), 64)
    spot = lambda q: (q // 8, pl.ds(aligned(8 * (q % 8)), 8))
    other.wait_recv()
    ph[...] = p_sum[me.core] + sb[...]
    y_sums = [send.copy(ph.at[:, quarter((me.y + k) % 4), :], yb.at[k - 1], upward[k - 1]) for k in (1, 2, 3)]
    start_edges(0, 0)
    take_edges(0, 2)
    take_edges(1, 0)
    take_edges(0, 1)
    take_edges(0, 3)
    for made in y_sums:
        made.wait_recv()
    pq[...] = ph[:, quarter(me.y), :] + yb[0] + yb[1] + yb[2]
    plane_sums = []
    for j, (q, peer) in enumerate(plane):
        c, rows = spot(q)
        plane_sums.append(send.copy(pq.at[c, rows, :], xzb.at[j], peer))
    take_relays(0)
    fold(1)
    take_edges(0, 0)
    for made in plane_sums:
        made.wait_recv()
    q = me.z * 4 + me.x
    c, rows = spot(q)
    total = pq[c, rows, :]
    for j in range(15):
        total = total + xzb[j]
    final_rows = pl.ds(aligned(64 * me.y + 8 * (q % 8)), 8)
    pout_ref[me.core, c, final_rows, :] = total
    spread = pout_ref.at[me.core, c, final_rows, :]
    plane_gather = [send.copy(spread, spread, peer) for _, peer in plane]
    finish(1)
    for made in plane_gather:
        made.wait_recv()
    spread_y = pout_ref.at[me.core, :, quarter(me.y), :]
    y_gather = [send.copy(spread_y, spread_y, peer) for peer in upward]
    fold(0)
    for made in y_gather:
        made.wait_recv()
    final = send.copy(pout_ref.at[me.core], pout_ref.at[me.core], sibling)
    finish(0)
    final.wait_recv()
    send.finish()


def shards(object_slices, probe_modes, prop_phase, background, positions, counts):
    lefts, rights, perm_pair = dft_constants()
    vmem = pl.BlockSpec(memory_space=pltpu.VMEM)
    square = (FRAME, FRAME)
    half_strip = (2, HALO, HALF)
    full_strip = (2, FRAME, HALF)
    tile = (STRIPS, 2, ROWS_EXT, HALF)
    blocks = (STRIPS, 2, ROWS_EXT // 8, 8, HALF)
    own = object_slices.reshape(SLICES, 2, FRAME // 8, 8, HALF)
    return pl.pallas_call(
        gradient_kernel,
        out_shape=(
            jax.ShapeDtypeStruct((SLICES,) + full_strip, F32),
            jax.ShapeDtypeStruct((MODES, 2) + square, F32),
        ),
        in_specs=[pl.BlockSpec(memory_space=pltpu.SMEM)] + [pl.BlockSpec(memory_space=pl.ANY)] * 8,
        out_specs=(vmem, vmem),
        scratch_shapes=[
            pltpu.VMEM(blocks, F32),
            pltpu.VMEM(blocks, F32),
            pltpu.VMEM(tile, F32),
            pltpu.VMEM(tile, F32),
            pltpu.VMEM((MODES, 2) + square, F32),
            pltpu.VMEM(square, F32),
            pltpu.VMEM(square, F32),
            pltpu.VMEM((2,) + square, jnp.int32),
            pltpu.VMEM((4, FRAME, 3 * FRAME), BF16),
            pltpu.VMEM((4, 3 * FRAME, FRAME), BF16),
            pltpu.VMEM((2,) + square, BF16),
            pltpu.VMEM((2, SLICES, 2) + square, F32),
            pltpu.VMEM((2,) + square, F32),
            pltpu.VMEM(square, F32),
            pltpu.VMEM((2,) + square, F32),
            pltpu.VMEM((2, MODES, 2) + square, F32),
            pltpu.VMEM((2, MODES, 2) + square, F32),
            pltpu.VMEM((MODES, 2, FRAME, 3 * FRAME), BF16),
            pltpu.VMEM((MODES, 2, 3 * FRAME, FRAME), BF16),
            pltpu.VMEM((MODES, 2) + square, F32),
            pltpu.VMEM((MODES, 2) + square, F32),
            pltpu.VMEM((2, FRAME + 16, FRAME), F32),
            pltpu.VMEM((2, 2, 4, PAD_ROWS // 8, 8, HALF), F32),
            pltpu.VMEM((2, 4, 2) + half_strip, F32),
            pltpu.VMEM((2, 4, 2) + half_strip, F32),
            pltpu.VMEM((2, 2, 2, FRAME, HALF), F32),
            pltpu.VMEM((2, 2, 2) + full_strip, F32),
            pltpu.VMEM((2,) + full_strip, F32),
            pltpu.VMEM((2,) + full_strip, F32),
            pltpu.VMEM((MODES, 2) + square, F32),
            pltpu.VMEM((2,) + square, F32),
            pltpu.VMEM((2,) + square, F32),
            pltpu.VMEM((3, 2, 64, FRAME), F32),
            pltpu.VMEM((2, 64, FRAME), F32),
            pltpu.VMEM((15, 8, FRAME), F32),
            pltpu.SemaphoreType.DMA((9,)),
            pltpu.SemaphoreType.DMA((COPIES,)),
            pltpu.SemaphoreType.DMA((COPIES,)),
        ],
        compiler_params=pltpu.CompilerParams(collective_id=1, has_side_effects=True, vmem_limit_bytes=60 << 20),
        name="gradient",
    )(positions, own, probe_modes, prop_phase, background, counts,
      jnp.asarray(lefts), jnp.asarray(rights), jnp.asarray(perm_pair))


def solution(mesh):
    in_specs = (
        P(None, None, "tile", "frame"),
        P(),
        P(),
        P(),
        P(("tile", "frame"), None),
        P(("tile", "frame"), None, None),
    )
    out_specs = (P(None, None, "tile", "frame"), P())
    return jax.shard_map(shards, mesh=mesh, in_specs=in_specs, out_specs=out_specs, check_vma=False)
```

```python
import numpy as np
import ml_dtypes
import jax
import jax.numpy as jnp
from jax import lax
from jax.experimental import pallas as pl
from jax.experimental.pallas import tpu as pltpu
from jax.sharding import PartitionSpec as P

FRAME = 256
HALF = 128
SLICES = 2
MODES = 2
HALO = 128
ROWS_EXT = 512
STRIPS = 8
WIN_COLS = 384
CHUNK = 32
TALL = 88
BLANK_ROWS = 248
PAD_ROWS = 2 * BLANK_ROWS + 264
F32 = jnp.float32
BF16 = jnp.bfloat16


def dft_constants():
    k = np.arange(HALF)[:, None]
    n = np.arange(HALF)[None, :]
    mats = []
    for odd in (0, 1):
        turns = ((2 * k + odd) * n) % FRAME
        angle = -2.0 * np.pi * turns / FRAME
        c, s = np.cos(angle) / 16.0, np.sin(angle) / 16.0
        mats.append(np.block([[c, -s], [s, c]]))
    even, odd = mats
    lefts, rights = [], []
    for m in (even, odd, even.T, odd.T):
        hi = m.astype(ml_dtypes.bfloat16)
        lo = (m - hi.astype(np.float64)).astype(ml_dtypes.bfloat16)
        lefts.append(np.concatenate([hi, hi, lo], axis=1))
        rights.append(np.concatenate([hi, hi, lo], axis=0))
    perm = np.zeros((FRAME, FRAME))
    order = np.concatenate([np.arange(0, FRAME, 2), np.arange(1, FRAME, 2)])
    perm[np.arange(FRAME), order] = 1.0
    perms = np.stack([perm, perm.T]).astype(ml_dtypes.bfloat16)
    return np.stack(lefts), np.stack(rights), perms


def mm(a, b):
    return jnp.dot(a, b, preferred_element_type=F32)


def parts3(x):
    a = x.astype(BF16)
    r = x - a.astype(F32)
    b = r.astype(BF16)
    c = (r - b.astype(F32)).astype(BF16)
    return a, b, c


def reorder_exact(x, perm, perm_t):
    a, b, c = parts3(x)
    y = mm(perm, a) + mm(perm, b) + mm(perm, c)
    a, b, c = parts3(y)
    return mm(a, perm_t) + mm(b, perm_t) + mm(c, perm_t)


def corner(pos_ref, f):
    r, c = pos_ref[f, 0], pos_ref[f, 1]
    block = jnp.minimum(r // 8, 31)
    cs = jnp.minimum(c // HALF, 5)
    return block, r - block * 8, cs, c - cs * HALF


MESH = pl.DeviceIdType.MESH


class Place:
    def __init__(self):
        tile, frame = lax.axis_index("tile"), lax.axis_index("frame")
        self.y, self.zl, self.core = tile // 4, (tile // 2) % 2, tile % 2
        self.zh, self.x = frame // 4, frame % 4
        self.z = self.zh * 2 + self.zl

    def at(self, y=None, zl=None, core=None, zh=None, x=None):
        pick = lambda given, own: own if given is None else given
        tile = (pick(y, self.y) * 2 + pick(zl, self.zl)) * 2 + pick(core, self.core)
        return tile, pick(zh, self.zh) * 4 + pick(x, self.x)

    def along_x(self, k):
        return self.at(x=(self.x + k) % 4)

    def along_y(self, k):
        return self.at(y=(self.y + k) % 4)

    def in_plane(self, j):
        q = (self.z * 4 + self.x + j) % 16
        z = q // 4
        return q, self.at(zl=z % 2, zh=z // 2, x=q % 4)

    def z_peer(self):
        return self.at(zh=1 - self.zh)

    def sibling(self):
        return self.at(core=1 - self.core)

    def outer(self):
        turn = self.core * self.zl + (1 - self.core) * (1 - self.zl)
        step = turn * (2 * self.core - 1)
        zh = turn * (1 - self.zh) + (1 - turn) * self.zh
        return self.at(y=(self.y + step + 4) % 4, zl=1 - self.zl, core=1 - self.core, zh=zh)


def greet(peers):
    barrier = pltpu.get_barrier_semaphore()
    for peer in peers:
        pl.semaphore_signal(barrier, inc=1, device_id=peer, device_id_type=MESH)
    pl.semaphore_wait(barrier, len(peers))


class Sender:
    def __init__(self, send_sems, recv_sems):
        self.send_sems, self.recv_sems = send_sems, recv_sems
        self.started = []

    def copy(self, src, dst, peer):
        n = len(self.started)
        made = pltpu.make_async_remote_copy(
            src_ref=src, dst_ref=dst, send_sem=self.send_sems.at[n], recv_sem=self.recv_sems.at[n],
            device_id=peer, device_id_type=MESH,
        )
        made.start()
        self.started.append(made)
        return made

    def finish(self):
        for made in self.started:
            made.wait_send()


def aligned(row):
    return pl.multiple_of(row, 8)


GATHER_COPIES = 6 + 4 + 8 + 16 + 4
SCATTER_COPIES = 32 + 8 + 16 + 2 + 1 + 3 + 15 + 15 + 3 + 1
COPIES = GATHER_COPIES + SCATTER_COPIES


def gradient_kernel(
    pos_ref, own_ref, probe_in, phase_in, back_in, counts_in, left_in, right_in, perm_in,
    out_ref, pout_ref,
    ext_0, ext_1, g_0, g_1, probe, phase_raw, back_raw, counts_raw, left, right, perms,
    obj, kern, bg, cnt, wave, u1, rop, lop, tmp, freq, padded, placed,
    edge_out, edge_sib, rb, xb, part, zb, p_sum, sb, ph, yb, pq, xzb,
    local_sems, send_sems, recv_sems,
):
    exts, gs = (ext_0, ext_1), (g_0, g_1)
    me = Place()
    f_own, f_other = me.zh * 4 + me.x, (1 - me.zh) * 4 + me.x
    sibling, outer, z_peer = me.sibling(), me.outer(), me.z_peer()
    ahead, behind = me.along_x(1), me.along_x(3)
    upward = [me.along_y(k) for k in (1, 2, 3)]
    plane = [me.in_plane(j) for j in range(1, 16)]

    loads = [
        pltpu.make_async_copy(src, dst, local_sems.at[n])
        for n, (src, dst) in enumerate((
            (perm_in, perms), (back_in, back_raw), (phase_in, phase_raw), (counts_in, counts_raw),
            (probe_in, probe), (left_in, left), (right_in, right),
        ))
    ]
    for load in loads:
        load.start()
    mine, own_blocks = pl.ds(HALO, FRAME), pl.ds(16, 32)
    keeps = [
        pltpu.make_async_copy(own_ref.at[s], exts[s].at[f_own, :, own_blocks], local_sems.at[len(loads) + s])
        for s in range(SLICES)
    ]
    for keep in keeps:
        keep.start()

    greet([sibling, outer] + upward + [peer for _, peer in plane])
    send = Sender(send_sems, recv_sems)

    out_src, out_dst = 16 + 16 * me.core, 48 * (1 - me.core)
    sib_src, sib_dst = 16 + 16 * (1 - me.core), 48 * me.core
    margins = ([], [])

    def pass_edges(strip, s, ref=None):
        base = exts[s].at[strip] if ref is None else ref.at[s]
        shift = 0 if ref is None else 16
        margins[s].append(send.copy(
            base.at[:, pl.ds(out_src - shift, 16)], exts[s].at[strip, :, pl.ds(out_dst, 16)], outer
        ))

    def pass_half(which, s):
        group = exts[s].at[pl.ds(half_of[which] * 4, 4)]
        margins[s].append(send.copy(
            group.at[:, :, pl.ds(sib_src, 16)], group.at[:, :, pl.ds(sib_dst, 16)], sibling
        ))

    to_z, to_x, relayed = {}, {}, {}
    own_half, other_half = 0, 1
    half_of = (me.zh, 1 - me.zh)

    def strip_at(which, k):
        return half_of[which] * 4 + (me.x + k + 4) % 4

    def own_to_z(s):
        to_z[s] = send.copy(own_ref.at[s], exts[s].at[f_own, :, own_blocks], z_peer)

    def own_to_x(s):
        to_x[own_half, s, 0] = send.copy(own_ref.at[s], exts[s].at[f_own, :, own_blocks], ahead)
        to_x[own_half, s, 1] = send.copy(own_ref.at[s], exts[s].at[f_own, :, own_blocks], behind)

    def from_z(s):
        to_z[s].wait_recv()
        whole = exts[s].at[f_other, :, own_blocks]
        to_x[other_half, s, 0] = send.copy(whole, whole, ahead)
        to_x[other_half, s, 1] = send.copy(whole, whole, behind)
        pass_edges(f_other, s)

    def from_x(which, s):
        for way, peer, k in ((0, ahead, -1), (1, behind, 1)):
            to_x[which, s, way].wait_recv()
            half = exts[s].at[strip_at(which, k), way, own_blocks]
            relayed[which, s, way] = send.copy(half, half, peer)
        for k in (-1, 1):
            pass_edges(strip_at(which, k), s)

    def from_relay(which, s):
        if which == own_half:
            keeps[s].wait()
        for way in range(2):
            relayed[which, s, way].wait_recv()
        pass_edges(strip_at(which, 2), s)
        pass_half(which, s)

    def cut(s):
        for made in margins[s]:
            made.wait_recv()

        @pl.loop(0, 2)
        def _(f):
            block, row_shift, cs, col_shift = corner(pos_ref, f)
            for p in range(2):
                for q in range(FRAME // CHUNK):
                    x = jnp.concatenate([
                        jnp.concatenate([exts[s][cs + j, p, block + q * CHUNK // 8 + n] for n in range(CHUNK // 8 + 1)], axis=0)
                        for j in range(3)
                    ], axis=1)
                    x = pltpu.roll(x, lax.rem(WIN_COLS - col_shift, WIN_COLS), 1)[:, :FRAME]
                    x = pltpu.roll(x, lax.rem(CHUNK + 8 - row_shift, CHUNK + 8), 0)
                    obj[f, s, p, pl.ds(q * CHUNK, CHUNK), :] = x[:CHUNK]

    def put_right(m, parity, rows, x):
        hi = x.astype(BF16)
        lo = (x - hi.astype(F32)).astype(BF16)
        rop[m, parity, rows, 0:256] = hi
        rop[m, parity, rows, 256:512] = lo
        rop[m, parity, rows, 512:768] = hi

    def put_left(m, parity, start, x):
        hi = x.astype(BF16)
        lo = (x - hi.astype(F32)).astype(BF16)
        n = x.shape[0]
        lop[m, parity, pl.ds(start, n), :] = hi
        lop[m, parity, pl.ds(256 + start, n), :] = lo
        lop[m, parity, pl.ds(512 + start, n), :] = hi

    def forward(m, produce):
        for q in range(FRAME // CHUNK):
            rows = pl.ds(q * CHUNK, CHUNK)
            re, im = produce(m, rows)
            a, b = re[:, :HALF], re[:, HALF:]
            c, d = im[:, :HALF], im[:, HALF:]
            put_right(m, 0, rows, jnp.concatenate([a + b, c + d], axis=1))
            put_right(m, 1, rows, jnp.concatenate([a - b, c - d], axis=1))
        tmp[m, 0] = mm(rop[m, 0], right[2])
        tmp[m, 1] = mm(rop[m, 1], right[3])
        yield
        for q in range(HALF // CHUNK):
            top = pl.ds(q * CHUNK, CHUNK)
            bot = pl.ds(HALF + q * CHUNK, CHUNK)
            et, eb = tmp[m, 0, top, :], tmp[m, 0, bot, :]
            ot, ob = tmp[m, 1, top, :], tmp[m, 1, bot, :]
            for parity, e, o in ((0, et + eb, ot + ob), (1, et - eb, ot - ob)):
                put_left(m, parity, q * CHUNK, jnp.concatenate([e[:, :HALF], o[:, :HALF]], axis=1))
                put_left(m, parity, HALF + q * CHUNK, jnp.concatenate([e[:, HALF:], o[:, HALF:]], axis=1))
        freq[m, 0] = mm(left[0], lop[m, 0])
        freq[m, 1] = mm(left[1], lop[m, 1])
        yield

    def backward(m, modify, consume):
        for parity in range(2):
            for q in range(HALF // CHUNK):
                top = pl.ds(q * CHUNK, CHUNK)
                bot = pl.ds(HALF + q * CHUNK, CHUNK)
                table_rows = pl.ds(parity * HALF + q * CHUNK, CHUNK)
                re, im = modify(table_rows, freq[m, parity, top, :], freq[m, parity, bot, :])
                put_left(m, parity, q * CHUNK, re)
                put_left(m, parity, HALF + q * CHUNK, im)
        tmp[m, 0] = mm(left[2], lop[m, 0])
        tmp[m, 1] = mm(left[3], lop[m, 1])
        yield
        for q in range(HALF // CHUNK):
            top = pl.ds(q * CHUNK, CHUNK)
            bot = pl.ds(HALF + q * CHUNK, CHUNK)
            gr, gi = tmp[m, 0, top, :], tmp[m, 0, bot, :]
            hr, hi = tmp[m, 1, top, :], tmp[m, 1, bot, :]
            for rows, re, im in ((top, gr + hr, gi + hi), (bot, gr - hr, gi - hi)):
                put_right(m, 0, rows, jnp.concatenate([re[:, :HALF], im[:, :HALF]], axis=1))
                put_right(m, 1, rows, jnp.concatenate([re[:, HALF:], im[:, HALF:]], axis=1))
        tmp[m, 0] = mm(rop[m, 0], right[0])
        tmp[m, 1] = mm(rop[m, 1], right[1])
        yield
        for q in range(FRAME // CHUNK):
            rows = pl.ds(q * CHUNK, CHUNK)
            g, h = tmp[m, 0, rows, :], tmp[m, 1, rows, :]
            re = jnp.concatenate([g[:, :HALF] + h[:, :HALF], g[:, :HALF] - h[:, :HALF]], axis=1)
            im = jnp.concatenate([g[:, HALF:] + h[:, HALF:], g[:, HALF:] - h[:, HALF:]], axis=1)
            consume(m, rows, re, im)

    def times(a_re, a_im, b_re, b_im):
        return a_re * b_re - a_im * b_im, a_re * b_im + a_im * b_re

    def conj_times(a_re, a_im, b_re, b_im):
        return a_re * b_re + a_im * b_im, a_re * b_im - a_im * b_re

    def pair(ref, *at):
        return ref[(*at[:-1], 0, at[-1], slice(None))], ref[(*at[:-1], 1, at[-1], slice(None))]

    def modes(*steps):
        def chain(m):
            for step in steps:
                yield from step(m)

        running = [chain(m) for m in range(MODES)]
        while running:
            running = [one for one in running if next(one, True) is None]

    def through_first_slice(f):
        def keep(m, rows, re, im):
            u1[f, m, 0, rows, :] = re
            u1[f, m, 1, rows, :] = im

        modes(lambda m: forward(m, lambda m, rows: times(*pair(probe, m, rows), *pair(obj, f, 0, rows))), lambda m: backward(m, lambda rows, re, im: times(kern[0, rows, :], kern[1, rows, :], re, im), keep))

    def keep_wave(f):
        def keep(m, rows, re, im):
            wave[f, m, 0, rows, :] = re
            wave[f, m, 1, rows, :] = im
        return keep

    def terms(f, incoming):
        _, row_shift, _, col_shift = corner(pos_ref, f)
        for q in range(FRAME // CHUNK):
            rows = pl.ds(q * CHUNK, CHUNK)
            total = None
            for m in range(MODES):
                one = conj_times(*incoming(m, rows), *pair(wave, f, m, rows))
                total = one if total is None else (total[0] + one[0], total[1] + one[1])
            for c in range(2):
                padded[c, pl.ds(8 + q * CHUNK, CHUNK), :] = total[c]
        beside = jnp.zeros((TALL, HALF), F32)
        for c in range(2):
            for q in range(264 // TALL):
                x = pltpu.roll(padded[c, pl.ds(q * TALL, TALL + 8), :], lax.rem(TALL + row_shift, TALL + 8), 0)[:TALL]
                x = pltpu.roll(jnp.concatenate([x, beside], axis=1), col_shift, 1)
                for j in range(3):
                    placed[f, c, j, pl.ds(BLANK_ROWS // 8 + q * TALL // 8, TALL // 8)] = x[:, j * HALF:(j + 1) * HALF].reshape(TALL // 8, 8, HALF)

    def collect(s):
        corners = [corner(pos_ref, f) for f in range(2)]

        @pl.loop(0, STRIPS)
        def _(i):
            spots = []
            for block, _, cs, _ in corners:
                j = i - cs
                inside = jnp.logical_and(j >= 0, j < 3)
                spots.append((jnp.where(inside, j, 3), BLANK_ROWS // 8 - block))
            for c in range(2):
                for n in range(ROWS_EXT // 8):
                    x, y = [placed[f, c, j, row + n] for f, (j, row) in enumerate(spots)]
                    gs[s][i, c, pl.ds(n * 8, 8), :] = x + y

    g_out_src, g_sib_src = aligned(384 * me.core), aligned(384 * (1 - me.core))
    g_out_rows, g_sib_rows = aligned(HALO + HALO * me.core), aligned(HALO + HALO * (1 - me.core))

    def strip(half, k):
        return half * 4 + (me.x + k) % 4

    edges, relays, crossing, last = {}, {}, {}, {}
    half_order = (1 - me.zh, me.zh)

    def start_edges(s, k):
        for h in range(2):
            i = strip(h, k)
            edges[s, k, h, 0] = send.copy(gs[s].at[i, :, pl.ds(g_out_src, HALO), :], edge_out.at[s, k, h], outer)
            edges[s, k, h, 1] = send.copy(gs[s].at[i, :, pl.ds(g_sib_src, HALO), :], edge_sib.at[s, k, h], sibling)

    def take_edges(s, k):
        g = gs[s]
        for h in range(2):
            edges[s, k, h, 0].wait_recv()
            edges[s, k, h, 1].wait_recv()
            i = strip(h, k)
            g[i, :, pl.ds(g_out_rows, HALO), :] += edge_out[s, k, h]
            g[i, :, pl.ds(g_sib_rows, HALO), :] += edge_sib[s, k, h]
        for n, h in enumerate(half_order):
            i = strip(h, k)
            if k == 2:
                relays[s, n, 0] = send.copy(g.at[i, 0, mine, :], rb.at[s, n, 0], ahead)
                relays[s, n, 1] = send.copy(g.at[i, 1, mine, :], rb.at[s, n, 1], behind)
            if k == 1:
                crossing[s, n, 0, 1] = send.copy(g.at[i, 1, mine, :], xb.at[s, n, 0, 1], ahead)
            if k == 3:
                crossing[s, n, 1, 0] = send.copy(g.at[i, 0, mine, :], xb.at[s, n, 1, 0], behind)

    def take_relays(s):
        for n, h in enumerate(half_order):
            for way, k, peer in ((0, 1, ahead), (1, 3, behind)):
                relays[s, n, way].wait_recv()
                i = strip(h, k)
                gs[s][i, way, mine, :] += rb[s, n, way]
                crossing[s, n, way, way] = send.copy(gs[s].at[i, way, mine, :], xb.at[s, n, way, way], peer)

    def take_crossing(s, n):
        for way in range(2):
            for c in range(2):
                crossing[s, n, way, c].wait_recv()
        return gs[s][strip(half_order[n], 0), :, mine, :] + xb[s, n, 0] + xb[s, n, 1]

    def fold(s):
        part[s] = take_crossing(s, 0)
        last[s] = send.copy(part.at[s], zb.at[s], z_peer)

    def finish(s):
        own_sum = take_crossing(s, 1)
        last[s].wait_recv()
        out_ref[s] = own_sum + zb[s]

    own_to_z(0)
    own_to_x(0)
    own_to_z(1)
    own_to_x(1)
    pass_edges(f_own, 0, own_ref)
    for load in loads[:4]:
        load.wait()
    perm, perm_t = perms[0], perms[1]
    bg[...] = reorder_exact(back_raw[...], perm, perm_t)
    phase = reorder_exact(phase_raw[...], perm, perm_t)
    from_z(0)
    from_x(own_half, 0)
    kern[0] = jnp.cos(phase)
    kern[1] = jnp.sin(phase)
    from_z(1)
    for f in range(2):
        half = mm(perm, counts_raw[f].astype(F32).astype(BF16)).astype(BF16)
        cnt[f] = mm(half, perm_t)
    from_x(own_half, 1)
    padded[...] = jnp.zeros_like(padded)
    placed[...] = jnp.zeros_like(placed)
    from_x(other_half, 0)
    from_relay(own_half, 0)
    from_relay(other_half, 0)
    pass_edges(f_own, 1, own_ref)
    for load in loads[4:]:
        load.wait()
    from_x(other_half, 1)
    from_relay(own_half, 1)
    cut(0)
    from_relay(other_half, 1)
    through_first_slice(0)
    through_first_slice(1)
    cut(1)

    @pl.loop(0, 2)
    def _(f):
        modes(lambda m: forward(m, lambda m, rows: times(*pair(u1, f, m, rows), *pair(obj, f, 1, rows))))
        for parity in range(2):
            for q in range(HALF // CHUNK):
                top = pl.ds(q * CHUNK, CHUNK)
                bot = pl.ds(HALF + q * CHUNK, CHUNK)
                rows = pl.ds(parity * HALF + q * CHUNK, CHUNK)
                level = bg[rows, :]
                for m in range(MODES):
                    re, im = freq[m, parity, top, :], freq[m, parity, bot, :]
                    level = level + re * re + im * im
                cnt[f, rows, :] = 1.0 - cnt[f, rows, :] / level
        modes(lambda m: backward(m, lambda rows, re, im: (re * cnt[f, rows, :], im * cnt[f, rows, :]), keep_wave(f)))
        terms(f, lambda m, rows: pair(u1, f, m, rows))

    collect(1)
    for k in (2, 1, 3, 0):
        start_edges(1, k)

    for f in range(2):
        modes(lambda m: forward(m, lambda m, rows: conj_times(*pair(obj, f, 1, rows), *pair(wave, f, m, rows))))
        if f == 0:
            take_edges(1, 2)
        else:
            take_relays(1)
        modes(lambda m: backward(m, lambda rows, re, im: conj_times(kern[0, rows, :], kern[1, rows, :], re, im), keep_wave(f)))
        if f == 0:
            take_edges(1, 1)
            take_edges(1, 3)
        terms(f, lambda m, rows: pair(probe, m, rows))
        for m in range(MODES):
            for q in range(FRAME // CHUNK):
                rows = pl.ds(q * CHUNK, CHUNK)
                re, im = conj_times(*pair(obj, f, 0, rows), *pair(wave, f, m, rows))
                if f == 0:
                    p_sum[m, 0, rows, :] = re
                    p_sum[m, 1, rows, :] = im
                else:
                    p_sum[m, 0, rows, :] += re
                    p_sum[m, 1, rows, :] += im

    other = send.copy(p_sum.at[1 - me.core], sb, sibling)
    collect(0)
    for k in (2, 1, 3):
        start_edges(0, k)
    quarter = lambda y: pl.ds(aligned(64 * y), 64)
    spot = lambda q: (q // 8, pl.ds(aligned(8 * (q % 8)), 8))
    other.wait_recv()
    ph[...] = p_sum[me.core] + sb[...]
    y_sums = [send.copy(ph.at[:, quarter((me.y + k) % 4), :], yb.at[k - 1], upward[k - 1]) for k in (1, 2, 3)]
    start_edges(0, 0)
    take_edges(0, 2)
    take_edges(1, 0)
    take_edges(0, 1)
    take_edges(0, 3)
    for made in y_sums:
        made.wait_recv()
    pq[...] = ph[:, quarter(me.y), :] + yb[0] + yb[1] + yb[2]
    plane_sums = []
    for j, (q, peer) in enumerate(plane):
        c, rows = spot(q)
        plane_sums.append(send.copy(pq.at[c, rows, :], xzb.at[j], peer))
    take_relays(0)
    fold(1)
    take_edges(0, 0)
    for made in plane_sums:
        made.wait_recv()
    q = me.z * 4 + me.x
    c, rows = spot(q)
    total = pq[c, rows, :]
    for j in range(15):
        total = total + xzb[j]
    final_rows = pl.ds(aligned(64 * me.y + 8 * (q % 8)), 8)
    pout_ref[me.core, c, final_rows, :] = total
    spread = pout_ref.at[me.core, c, final_rows, :]
    plane_gather = [send.copy(spread, spread, peer) for _, peer in plane]
    finish(1)
    for made in plane_gather:
        made.wait_recv()
    spread_y = pout_ref.at[me.core, :, quarter(me.y), :]
    y_gather = [send.copy(spread_y, spread_y, peer) for peer in upward]
    fold(0)
    for made in y_gather:
        made.wait_recv()
    final = send.copy(pout_ref.at[me.core], pout_ref.at[me.core], sibling)
    finish(0)
    final.wait_recv()
    send.finish()


def shards(object_slices, probe_modes, prop_phase, background, positions, counts):
    lefts, rights, perm_pair = dft_constants()
    vmem = pl.BlockSpec(memory_space=pltpu.VMEM)
    square = (FRAME, FRAME)
    half_strip = (2, HALO, HALF)
    full_strip = (2, FRAME, HALF)
    tile = (STRIPS, 2, ROWS_EXT, HALF)
    blocks = (STRIPS, 2, ROWS_EXT // 8, 8, HALF)
    own = object_slices.reshape(SLICES, 2, FRAME // 8, 8, HALF)
    return pl.pallas_call(
        gradient_kernel,
        out_shape=(
            jax.ShapeDtypeStruct((SLICES,) + full_strip, F32),
            jax.ShapeDtypeStruct((MODES, 2) + square, F32),
        ),
        in_specs=[pl.BlockSpec(memory_space=pltpu.SMEM)] + [pl.BlockSpec(memory_space=pl.ANY)] * 8,
        out_specs=(vmem, vmem),
        scratch_shapes=[
            pltpu.VMEM(blocks, F32),
            pltpu.VMEM(blocks, F32),
            pltpu.VMEM(tile, F32),
            pltpu.VMEM(tile, F32),
            pltpu.VMEM((MODES, 2) + square, F32),
            pltpu.VMEM(square, F32),
            pltpu.VMEM(square, F32),
            pltpu.VMEM((2,) + square, jnp.int32),
            pltpu.VMEM((4, FRAME, 3 * FRAME), BF16),
            pltpu.VMEM((4, 3 * FRAME, FRAME), BF16),
            pltpu.VMEM((2,) + square, BF16),
            pltpu.VMEM((2, SLICES, 2) + square, F32),
            pltpu.VMEM((2,) + square, F32),
            pltpu.VMEM(square, F32),
            pltpu.VMEM((2,) + square, F32),
            pltpu.VMEM((2, MODES, 2) + square, F32),
            pltpu.VMEM((2, MODES, 2) + square, F32),
            pltpu.VMEM((MODES, 2, FRAME, 3 * FRAME), BF16),
            pltpu.VMEM((MODES, 2, 3 * FRAME, FRAME), BF16),
            pltpu.VMEM((MODES, 2) + square, F32),
            pltpu.VMEM((MODES, 2) + square, F32),
            pltpu.VMEM((2, FRAME + 16, FRAME), F32),
            pltpu.VMEM((2, 2, 4, PAD_ROWS // 8, 8, HALF), F32),
            pltpu.VMEM((2, 4, 2) + half_strip, F32),
            pltpu.VMEM((2, 4, 2) + half_strip, F32),
            pltpu.VMEM((2, 2, 2, FRAME, HALF), F32),
            pltpu.VMEM((2, 2, 2) + full_strip, F32),
            pltpu.VMEM((2,) + full_strip, F32),
            pltpu.VMEM((2,) + full_strip, F32),
            pltpu.VMEM((MODES, 2) + square, F32),
            pltpu.VMEM((2,) + square, F32),
            pltpu.VMEM((2,) + square, F32),
            pltpu.VMEM((3, 2, 64, FRAME), F32),
            pltpu.VMEM((2, 64, FRAME), F32),
            pltpu.VMEM((15, 8, FRAME), F32),
            pltpu.SemaphoreType.DMA((9,)),
            pltpu.SemaphoreType.DMA((COPIES,)),
            pltpu.SemaphoreType.DMA((COPIES,)),
        ],
        compiler_params=pltpu.CompilerParams(collective_id=1, has_side_effects=True, vmem_limit_bytes=60 << 20),
        name="gradient",
    )(positions, own, probe_modes, prop_phase, background, counts,
      jnp.asarray(lefts), jnp.asarray(rights), jnp.asarray(perm_pair))


def solution(mesh):
    in_specs = (
        P(None, None, "tile", "frame"),
        P(),
        P(),
        P(),
        P(("tile", "frame"), None),
        P(("tile", "frame"), None, None),
    )
    out_specs = (P(None, None, "tile", "frame"), P())
    return jax.shard_map(shards, mesh=mesh, in_specs=in_specs, out_specs=out_specs, check_vma=False)
```

```python
import numpy as np
import ml_dtypes
import jax
import jax.numpy as jnp
from jax import lax
from jax.experimental import pallas as pl
from jax.experimental.pallas import tpu as pltpu
from jax.sharding import PartitionSpec as P

FRAME = 256
HALF = 128
SLICES = 2
MODES = 2
HALO = 128
ROWS_EXT = 512
STRIPS = 8
WIN_COLS = 384
CHUNK = 32
TALL = 88
BLANK_ROWS = 248
PAD_ROWS = 2 * BLANK_ROWS + 264
F32 = jnp.float32
BF16 = jnp.bfloat16


def dft_constants():
    k = np.arange(HALF)[:, None]
    n = np.arange(HALF)[None, :]
    mats = []
    for odd in (0, 1):
        turns = ((2 * k + odd) * n) % FRAME
        angle = -2.0 * np.pi * turns / FRAME
        c, s = np.cos(angle) / 16.0, np.sin(angle) / 16.0
        mats.append(np.block([[c, -s], [s, c]]))
    even, odd = mats
    lefts, rights = [], []
    for m in (even, odd, even.T, odd.T):
        hi = m.astype(ml_dtypes.bfloat16)
        lo = (m - hi.astype(np.float64)).astype(ml_dtypes.bfloat16)
        lefts.append(np.concatenate([hi, hi, lo], axis=1))
        rights.append(np.concatenate([hi, hi, lo], axis=0))
    perm = np.zeros((FRAME, FRAME))
    order = np.concatenate([np.arange(0, FRAME, 2), np.arange(1, FRAME, 2)])
    perm[np.arange(FRAME), order] = 1.0
    perms = np.stack([perm, perm.T]).astype(ml_dtypes.bfloat16)
    return np.stack(lefts), np.stack(rights), perms


def mm(a, b):
    return jnp.dot(a, b, preferred_element_type=F32)


def parts3(x):
    a = x.astype(BF16)
    r = x - a.astype(F32)
    b = r.astype(BF16)
    c = (r - b.astype(F32)).astype(BF16)
    return a, b, c


def reorder_exact(x, perm, perm_t):
    a, b, c = parts3(x)
    y = mm(perm, a) + mm(perm, b) + mm(perm, c)
    a, b, c = parts3(y)
    return mm(a, perm_t) + mm(b, perm_t) + mm(c, perm_t)


def corner(pos_ref, f):
    r, c = pos_ref[f, 0], pos_ref[f, 1]
    block = jnp.minimum(r // 8, 31)
    cs = jnp.minimum(c // HALF, 5)
    return block, r - block * 8, cs, c - cs * HALF


MESH = pl.DeviceIdType.MESH


class Place:
    def __init__(self):
        tile, frame = lax.axis_index("tile"), lax.axis_index("frame")
        self.y, self.zl, self.core = tile // 4, (tile // 2) % 2, tile % 2
        self.zh, self.x = frame // 4, frame % 4
        self.z = self.zh * 2 + self.zl

    def at(self, y=None, zl=None, core=None, zh=None, x=None):
        pick = lambda given, own: own if given is None else given
        tile = (pick(y, self.y) * 2 + pick(zl, self.zl)) * 2 + pick(core, self.core)
        return tile, pick(zh, self.zh) * 4 + pick(x, self.x)

    def along_x(self, k):
        return self.at(x=(self.x + k) % 4)

    def along_y(self, k):
        return self.at(y=(self.y + k) % 4)

    def in_plane(self, j):
        q = (self.z * 4 + self.x + j) % 16
        z = q // 4
        return q, self.at(zl=z % 2, zh=z // 2, x=q % 4)

    def z_peer(self):
        return self.at(zh=1 - self.zh)

    def sibling(self):
        return self.at(core=1 - self.core)

    def outer(self):
        turn = self.core * self.zl + (1 - self.core) * (1 - self.zl)
        step = turn * (2 * self.core - 1)
        zh = turn * (1 - self.zh) + (1 - turn) * self.zh
        return self.at(y=(self.y + step + 4) % 4, zl=1 - self.zl, core=1 - self.core, zh=zh)


def greet(peers):
    barrier = pltpu.get_barrier_semaphore()
    for peer in peers:
        pl.semaphore_signal(barrier, inc=1, device_id=peer, device_id_type=MESH)
    pl.semaphore_wait(barrier, len(peers))


class Sender:
    def __init__(self, send_sems, recv_sems):
        self.send_sems, self.recv_sems = send_sems, recv_sems
        self.started = []

    def copy(self, src, dst, peer):
        n = len(self.started)
        made = pltpu.make_async_remote_copy(
            src_ref=src, dst_ref=dst, send_sem=self.send_sems.at[n], recv_sem=self.recv_sems.at[n],
            device_id=peer, device_id_type=MESH,
        )
        made.start()
        self.started.append(made)
        return made

    def finish(self):
        for made in self.started:
            made.wait_send()


def aligned(row):
    return pl.multiple_of(row, 8)


GATHER_COPIES = 6 + 4 + 8 + 16 + 4
SCATTER_COPIES = 32 + 8 + 16 + 2 + 1 + 3 + 15 + 15 + 3 + 1
COPIES = GATHER_COPIES + SCATTER_COPIES


def gradient_kernel(
    pos_ref, own_ref, probe_in, phase_in, back_in, counts_in, left_in, right_in, perm_in,
    out_ref, zb, pout_ref,
    ext_0, ext_1, g_0, g_1, probe, phase_raw, back_raw, counts_raw, left, right, perms,
    obj, kern, bg, cnt, wave, u1, rop, lop, tmp, freq, padded, placed,
    edge_out, edge_sib, rb, xb, part, p_sum, sb, ph, yb, pq, xzb,
    local_sems, send_sems, recv_sems,
):
    exts, gs = (ext_0, ext_1), (g_0, g_1)
    me = Place()
    f_own, f_other = me.zh * 4 + me.x, (1 - me.zh) * 4 + me.x
    sibling, outer, z_peer = me.sibling(), me.outer(), me.z_peer()
    ahead, behind = me.along_x(1), me.along_x(3)
    upward = [me.along_y(k) for k in (1, 2, 3)]
    plane = [me.in_plane(j) for j in range(1, 16)]

    loads = [
        pltpu.make_async_copy(src, dst, local_sems.at[n])
        for n, (src, dst) in enumerate((
            (perm_in, perms), (back_in, back_raw), (phase_in, phase_raw), (counts_in, counts_raw),
            (probe_in, probe), (left_in, left), (right_in, right),
        ))
    ]
    for load in loads:
        load.start()
    mine, own_blocks = pl.ds(HALO, FRAME), pl.ds(16, 32)
    keeps = [
        pltpu.make_async_copy(own_ref.at[s], exts[s].at[f_own, :, own_blocks], local_sems.at[len(loads) + s])
        for s in range(SLICES)
    ]
    for keep in keeps:
        keep.start()

    greet([sibling, outer] + upward + [peer for _, peer in plane])
    send = Sender(send_sems, recv_sems)

    out_src, out_dst = 16 + 16 * me.core, 48 * (1 - me.core)
    sib_src, sib_dst = 16 + 16 * (1 - me.core), 48 * me.core
    margins = ([], [])

    def pass_edges(strip, s, ref=None):
        base = exts[s].at[strip] if ref is None else ref.at[s]
        shift = 0 if ref is None else 16
        margins[s].append(send.copy(
            base.at[:, pl.ds(out_src - shift, 16)], exts[s].at[strip, :, pl.ds(out_dst, 16)], outer
        ))

    def pass_half(which, s):
        group = exts[s].at[pl.ds(half_of[which] * 4, 4)]
        margins[s].append(send.copy(
            group.at[:, :, pl.ds(sib_src, 16)], group.at[:, :, pl.ds(sib_dst, 16)], sibling
        ))

    to_z, to_x, relayed = {}, {}, {}
    own_half, other_half = 0, 1
    half_of = (me.zh, 1 - me.zh)

    def strip_at(which, k):
        return half_of[which] * 4 + (me.x + k + 4) % 4

    def own_to_z(s):
        to_z[s] = send.copy(own_ref.at[s], exts[s].at[f_own, :, own_blocks], z_peer)

    def own_to_x(s):
        to_x[own_half, s, 0] = send.copy(own_ref.at[s], exts[s].at[f_own, :, own_blocks], ahead)
        to_x[own_half, s, 1] = send.copy(own_ref.at[s], exts[s].at[f_own, :, own_blocks], behind)

    def from_z(s):
        to_z[s].wait_recv()
        whole = exts[s].at[f_other, :, own_blocks]
        to_x[other_half, s, 0] = send.copy(whole, whole, ahead)
        to_x[other_half, s, 1] = send.copy(whole, whole, behind)
        pass_edges(f_other, s)

    def from_x(which, s):
        for way, peer, k in ((0, ahead, -1), (1, behind, 1)):
            to_x[which, s, way].wait_recv()
            half = exts[s].at[strip_at(which, k), way, own_blocks]
            relayed[which, s, way] = send.copy(half, half, peer)
        for k in (-1, 1):
            pass_edges(strip_at(which, k), s)

    def from_relay(which, s):
        if which == own_half:
            keeps[s].wait()
        for way in range(2):
            relayed[which, s, way].wait_recv()
        pass_edges(strip_at(which, 2), s)
        pass_half(which, s)

    def cut(s):
        for made in margins[s]:
            made.wait_recv()

        @pl.loop(0, 2)
        def _(f):
            block, row_shift, cs, col_shift = corner(pos_ref, f)
            for p in range(2):
                for q in range(FRAME // CHUNK):
                    x = jnp.concatenate([
                        jnp.concatenate([exts[s][cs + j, p, block + q * CHUNK // 8 + n] for n in range(CHUNK // 8 + 1)], axis=0)
                        for j in range(3)
                    ], axis=1)
                    x = pltpu.roll(x, lax.rem(WIN_COLS - col_shift, WIN_COLS), 1)[:, :FRAME]
                    x = pltpu.roll(x, lax.rem(CHUNK + 8 - row_shift, CHUNK + 8), 0)
                    obj[f, s, p, pl.ds(q * CHUNK, CHUNK), :] = x[:CHUNK]

    def put_right(m, parity, rows, x):
        hi = x.astype(BF16)
        lo = (x - hi.astype(F32)).astype(BF16)
        rop[m, parity, rows, 0:256] = hi
        rop[m, parity, rows, 256:512] = lo
        rop[m, parity, rows, 512:768] = hi

    def put_left(m, parity, start, x):
        hi = x.astype(BF16)
        lo = (x - hi.astype(F32)).astype(BF16)
        n = x.shape[0]
        lop[m, parity, pl.ds(start, n), :] = hi
        lop[m, parity, pl.ds(256 + start, n), :] = lo
        lop[m, parity, pl.ds(512 + start, n), :] = hi

    def forward(m, produce):
        for q in range(FRAME // CHUNK):
            rows = pl.ds(q * CHUNK, CHUNK)
            re, im = produce(m, rows)
            a, b = re[:, :HALF], re[:, HALF:]
            c, d = im[:, :HALF], im[:, HALF:]
            put_right(m, 0, rows, jnp.concatenate([a + b, c + d], axis=1))
            put_right(m, 1, rows, jnp.concatenate([a - b, c - d], axis=1))
        tmp[m, 0] = mm(rop[m, 0], right[2])
        tmp[m, 1] = mm(rop[m, 1], right[3])
        yield
        for q in range(HALF // CHUNK):
            top = pl.ds(q * CHUNK, CHUNK)
            bot = pl.ds(HALF + q * CHUNK, CHUNK)
            et, eb = tmp[m, 0, top, :], tmp[m, 0, bot, :]
            ot, ob = tmp[m, 1, top, :], tmp[m, 1, bot, :]
            for parity, e, o in ((0, et + eb, ot + ob), (1, et - eb, ot - ob)):
                put_left(m, parity, q * CHUNK, jnp.concatenate([e[:, :HALF], o[:, :HALF]], axis=1))
                put_left(m, parity, HALF + q * CHUNK, jnp.concatenate([e[:, HALF:], o[:, HALF:]], axis=1))
        freq[m, 0] = mm(left[0], lop[m, 0])
        freq[m, 1] = mm(left[1], lop[m, 1])
        yield

    def backward(m, modify, consume):
        for parity in range(2):
            for q in range(HALF // CHUNK):
                top = pl.ds(q * CHUNK, CHUNK)
                bot = pl.ds(HALF + q * CHUNK, CHUNK)
                table_rows = pl.ds(parity * HALF + q * CHUNK, CHUNK)
                re, im = modify(table_rows, freq[m, parity, top, :], freq[m, parity, bot, :])
                put_left(m, parity, q * CHUNK, re)
                put_left(m, parity, HALF + q * CHUNK, im)
        tmp[m, 0] = mm(left[2], lop[m, 0])
        tmp[m, 1] = mm(left[3], lop[m, 1])
        yield
        for q in range(HALF // CHUNK):
            top = pl.ds(q * CHUNK, CHUNK)
            bot = pl.ds(HALF + q * CHUNK, CHUNK)
            gr, gi = tmp[m, 0, top, :], tmp[m, 0, bot, :]
            hr, hi = tmp[m, 1, top, :], tmp[m, 1, bot, :]
            for rows, re, im in ((top, gr + hr, gi + hi), (bot, gr - hr, gi - hi)):
                put_right(m, 0, rows, jnp.concatenate([re[:, :HALF], im[:, :HALF]], axis=1))
                put_right(m, 1, rows, jnp.concatenate([re[:, HALF:], im[:, HALF:]], axis=1))
        tmp[m, 0] = mm(rop[m, 0], right[0])
        tmp[m, 1] = mm(rop[m, 1], right[1])
        yield
        for q in range(FRAME // CHUNK):
            rows = pl.ds(q * CHUNK, CHUNK)
            g, h = tmp[m, 0, rows, :], tmp[m, 1, rows, :]
            re = jnp.concatenate([g[:, :HALF] + h[:, :HALF], g[:, :HALF] - h[:, :HALF]], axis=1)
            im = jnp.concatenate([g[:, HALF:] + h[:, HALF:], g[:, HALF:] - h[:, HALF:]], axis=1)
            consume(m, rows, re, im)

    def times(a_re, a_im, b_re, b_im):
        return a_re * b_re - a_im * b_im, a_re * b_im + a_im * b_re

    def conj_times(a_re, a_im, b_re, b_im):
        return a_re * b_re + a_im * b_im, a_re * b_im - a_im * b_re

    def pair(ref, *at):
        return ref[(*at[:-1], 0, at[-1], slice(None))], ref[(*at[:-1], 1, at[-1], slice(None))]

    def modes(*steps):
        def chain(m):
            for step in steps:
                yield from step(m)

        running = [chain(m) for m in range(MODES)]
        while running:
            running = [one for one in running if next(one, True) is None]

    def through_first_slice(f):
        def keep(m, rows, re, im):
            u1[f, m, 0, rows, :] = re
            u1[f, m, 1, rows, :] = im

        modes(lambda m: forward(m, lambda m, rows: times(*pair(probe, m, rows), *pair(obj, f, 0, rows))), lambda m: backward(m, lambda rows, re, im: times(kern[0, rows, :], kern[1, rows, :], re, im), keep))

    def keep_wave(f):
        def keep(m, rows, re, im):
            wave[f, m, 0, rows, :] = re
            wave[f, m, 1, rows, :] = im
        return keep

    def terms(f, incoming):
        _, row_shift, _, col_shift = corner(pos_ref, f)
        for q in range(FRAME // CHUNK):
            rows = pl.ds(q * CHUNK, CHUNK)
            total = None
            for m in range(MODES):
                one = conj_times(*incoming(m, rows), *pair(wave, f, m, rows))
                total = one if total is None else (total[0] + one[0], total[1] + one[1])
            for c in range(2):
                padded[c, pl.ds(8 + q * CHUNK, CHUNK), :] = total[c]
        beside = jnp.zeros((TALL, HALF), F32)
        for c in range(2):
            for q in range(264 // TALL):
                x = pltpu.roll(padded[c, pl.ds(q * TALL, TALL + 8), :], lax.rem(TALL + row_shift, TALL + 8), 0)[:TALL]
                x = pltpu.roll(jnp.concatenate([x, beside], axis=1), col_shift, 1)
                for j in range(3):
                    placed[f, c, j, pl.ds(BLANK_ROWS // 8 + q * TALL // 8, TALL // 8)] = x[:, j * HALF:(j + 1) * HALF].reshape(TALL // 8, 8, HALF)

    def collect(s):
        corners = [corner(pos_ref, f) for f in range(2)]

        @pl.loop(0, STRIPS)
        def _(i):
            spots = []
            for block, _, cs, _ in corners:
                j = i - cs
                inside = jnp.logical_and(j >= 0, j < 3)
                spots.append((jnp.where(inside, j, 3), BLANK_ROWS // 8 - block))
            for c in range(2):
                for n in range(ROWS_EXT // 8):
                    x, y = [placed[f, c, j, row + n] for f, (j, row) in enumerate(spots)]
                    gs[s][i, c, pl.ds(n * 8, 8), :] = x + y

    g_out_src, g_sib_src = aligned(384 * me.core), aligned(384 * (1 - me.core))
    g_out_rows, g_sib_rows = aligned(HALO + HALO * me.core), aligned(HALO + HALO * (1 - me.core))

    def strip(half, k):
        return half * 4 + (me.x + k) % 4

    edges, relays, crossing, last = {}, {}, {}, {}
    half_order = (1 - me.zh, me.zh)

    def start_edges(s, k):
        for h in range(2):
            i = strip(h, k)
            edges[s, k, h, 0] = send.copy(gs[s].at[i, :, pl.ds(g_out_src, HALO), :], edge_out.at[s, k, h], outer)
            edges[s, k, h, 1] = send.copy(gs[s].at[i, :, pl.ds(g_sib_src, HALO), :], edge_sib.at[s, k, h], sibling)

    def take_edges(s, k):
        g = gs[s]
        for h in range(2):
            edges[s, k, h, 0].wait_recv()
            edges[s, k, h, 1].wait_recv()
            i = strip(h, k)
            g[i, :, pl.ds(g_out_rows, HALO), :] += edge_out[s, k, h]
            g[i, :, pl.ds(g_sib_rows, HALO), :] += edge_sib[s, k, h]
        for n, h in enumerate(half_order):
            i = strip(h, k)
            if k == 2:
                relays[s, n, 0] = send.copy(g.at[i, 0, mine, :], rb.at[s, n, 0], ahead)
                relays[s, n, 1] = send.copy(g.at[i, 1, mine, :], rb.at[s, n, 1], behind)
            if k == 1:
                crossing[s, n, 0, 1] = send.copy(g.at[i, 1, mine, :], xb.at[s, n, 0, 1], ahead)
            if k == 3:
                crossing[s, n, 1, 0] = send.copy(g.at[i, 0, mine, :], xb.at[s, n, 1, 0], behind)

    def take_relays(s):
        for n, h in enumerate(half_order):
            for way, k, peer in ((0, 1, ahead), (1, 3, behind)):
                relays[s, n, way].wait_recv()
                i = strip(h, k)
                gs[s][i, way, mine, :] += rb[s, n, way]
                crossing[s, n, way, way] = send.copy(gs[s].at[i, way, mine, :], xb.at[s, n, way, way], peer)

    def take_crossing(s, n):
        for way in range(2):
            for c in range(2):
                crossing[s, n, way, c].wait_recv()
        return gs[s][strip(half_order[n], 0), :, mine, :] + xb[s, n, 0] + xb[s, n, 1]

    def fold(s):
        part[s] = take_crossing(s, 0)
        last[s] = send.copy(part.at[s], zb.at[s], z_peer)

    def finish(s):
        out_ref[s] = take_crossing(s, 1)
        last[s].wait_recv()

    own_to_z(0)
    own_to_x(0)
    own_to_z(1)
    own_to_x(1)
    pass_edges(f_own, 0, own_ref)
    for load in loads[:4]:
        load.wait()
    perm, perm_t = perms[0], perms[1]
    bg[...] = reorder_exact(back_raw[...], perm, perm_t)
    phase = reorder_exact(phase_raw[...], perm, perm_t)
    from_z(0)
    from_x(own_half, 0)
    kern[0] = jnp.cos(phase)
    kern[1] = jnp.sin(phase)
    from_z(1)
    for f in range(2):
        half = mm(perm, counts_raw[f].astype(F32).astype(BF16)).astype(BF16)
        cnt[f] = mm(half, perm_t)
    from_x(own_half, 1)
    padded[...] = jnp.zeros_like(padded)
    placed[...] = jnp.zeros_like(placed)
    from_x(other_half, 0)
    from_relay(own_half, 0)
    from_relay(other_half, 0)
    pass_edges(f_own, 1, own_ref)
    for load in loads[4:]:
        load.wait()
    from_x(other_half, 1)
    from_relay(own_half, 1)
    cut(0)
    from_relay(other_half, 1)
    through_first_slice(0)
    through_first_slice(1)
    cut(1)

    @pl.loop(0, 2)
    def _(f):
        modes(lambda m: forward(m, lambda m, rows: times(*pair(u1, f, m, rows), *pair(obj, f, 1, rows))))
        for parity in range(2):
            for q in range(HALF // CHUNK):
                top = pl.ds(q * CHUNK, CHUNK)
                bot = pl.ds(HALF + q * CHUNK, CHUNK)
                rows = pl.ds(parity * HALF + q * CHUNK, CHUNK)
                level = bg[rows, :]
                for m in range(MODES):
                    re, im = freq[m, parity, top, :], freq[m, parity, bot, :]
                    level = level + re * re + im * im
                cnt[f, rows, :] = 1.0 - cnt[f, rows, :] / level
        modes(lambda m: backward(m, lambda rows, re, im: (re * cnt[f, rows, :], im * cnt[f, rows, :]), keep_wave(f)))
        terms(f, lambda m, rows: pair(u1, f, m, rows))

    collect(1)
    for k in (2, 1, 3, 0):
        start_edges(1, k)

    for f in range(2):
        modes(lambda m: forward(m, lambda m, rows: conj_times(*pair(obj, f, 1, rows), *pair(wave, f, m, rows))))
        if f == 0:
            take_edges(1, 2)
        else:
            take_relays(1)
        modes(lambda m: backward(m, lambda rows, re, im: conj_times(kern[0, rows, :], kern[1, rows, :], re, im), keep_wave(f)))
        if f == 0:
            take_edges(1, 1)
            take_edges(1, 3)
        terms(f, lambda m, rows: pair(probe, m, rows))
        for m in range(MODES):
            for q in range(FRAME // CHUNK):
                rows = pl.ds(q * CHUNK, CHUNK)
                re, im = conj_times(*pair(obj, f, 0, rows), *pair(wave, f, m, rows))
                if f == 0:
                    p_sum[m, 0, rows, :] = re
                    p_sum[m, 1, rows, :] = im
                else:
                    p_sum[m, 0, rows, :] += re
                    p_sum[m, 1, rows, :] += im

    other = send.copy(p_sum.at[1 - me.core], sb, sibling)
    collect(0)
    for k in (2, 1, 3):
        start_edges(0, k)
    quarter = lambda y: pl.ds(aligned(64 * y), 64)
    spot = lambda q: (q // 8, pl.ds(aligned(8 * (q % 8)), 8))
    other.wait_recv()
    ph[...] = p_sum[me.core] + sb[...]
    y_sums = [send.copy(ph.at[:, quarter((me.y + k) % 4), :], yb.at[k - 1], upward[k - 1]) for k in (1, 2, 3)]
    start_edges(0, 0)
    take_edges(0, 2)
    take_edges(1, 0)
    take_edges(0, 1)
    take_edges(0, 3)
    for made in y_sums:
        made.wait_recv()
    pq[...] = ph[:, quarter(me.y), :] + yb[0] + yb[1] + yb[2]
    plane_sums = []
    for j, (q, peer) in enumerate(plane):
        c, rows = spot(q)
        plane_sums.append(send.copy(pq.at[c, rows, :], xzb.at[j], peer))
    take_relays(0)
    fold(1)
    take_edges(0, 0)
    for made in plane_sums:
        made.wait_recv()
    q = me.z * 4 + me.x
    c, rows = spot(q)
    total = pq[c, rows, :]
    for j in range(15):
        total = total + xzb[j]
    final_rows = pl.ds(aligned(64 * me.y + 8 * (q % 8)), 8)
    pout_ref[me.core, c, final_rows, :] = total
    spread = pout_ref.at[me.core, c, final_rows, :]
    plane_gather = [send.copy(spread, spread, peer) for _, peer in plane]
    finish(1)
    for made in plane_gather:
        made.wait_recv()
    spread_y = pout_ref.at[me.core, :, quarter(me.y), :]
    y_gather = [send.copy(spread_y, spread_y, peer) for peer in upward]
    fold(0)
    for made in y_gather:
        made.wait_recv()
    final = send.copy(pout_ref.at[me.core], pout_ref.at[me.core], sibling)
    finish(0)
    final.wait_recv()
    send.finish()


def shards(object_slices, probe_modes, prop_phase, background, positions, counts):
    lefts, rights, perm_pair = dft_constants()
    vmem = pl.BlockSpec(memory_space=pltpu.VMEM)
    square = (FRAME, FRAME)
    half_strip = (2, HALO, HALF)
    full_strip = (2, FRAME, HALF)
    tile = (STRIPS, 2, ROWS_EXT, HALF)
    blocks = (STRIPS, 2, ROWS_EXT // 8, 8, HALF)
    own = object_slices.reshape(SLICES, 2, FRAME // 8, 8, HALF)
    near, far, probe_grad = pl.pallas_call(
        gradient_kernel,
        out_shape=(
            jax.ShapeDtypeStruct((SLICES,) + full_strip, F32),
            jax.ShapeDtypeStruct((SLICES,) + full_strip, F32),
            jax.ShapeDtypeStruct((MODES, 2) + square, F32),
        ),
        in_specs=[pl.BlockSpec(memory_space=pltpu.SMEM)] + [pl.BlockSpec(memory_space=pl.ANY)] * 8,
        out_specs=(vmem, vmem, vmem),
        scratch_shapes=[
            pltpu.VMEM(blocks, F32),
            pltpu.VMEM(blocks, F32),
            pltpu.VMEM(tile, F32),
            pltpu.VMEM(tile, F32),
            pltpu.VMEM((MODES, 2) + square, F32),
            pltpu.VMEM(square, F32),
            pltpu.VMEM(square, F32),
            pltpu.VMEM((2,) + square, jnp.int32),
            pltpu.VMEM((4, FRAME, 3 * FRAME), BF16),
            pltpu.VMEM((4, 3 * FRAME, FRAME), BF16),
            pltpu.VMEM((2,) + square, BF16),
            pltpu.VMEM((2, SLICES, 2) + square, F32),
            pltpu.VMEM((2,) + square, F32),
            pltpu.VMEM(square, F32),
            pltpu.VMEM((2,) + square, F32),
            pltpu.VMEM((2, MODES, 2) + square, F32),
            pltpu.VMEM((2, MODES, 2) + square, F32),
            pltpu.VMEM((MODES, 2, FRAME, 3 * FRAME), BF16),
            pltpu.VMEM((MODES, 2, 3 * FRAME, FRAME), BF16),
            pltpu.VMEM((MODES, 2) + square, F32),
            pltpu.VMEM((MODES, 2) + square, F32),
            pltpu.VMEM((2, FRAME + 16, FRAME), F32),
            pltpu.VMEM((2, 2, 4, PAD_ROWS // 8, 8, HALF), F32),
            pltpu.VMEM((2, 4, 2) + half_strip, F32),
            pltpu.VMEM((2, 4, 2) + half_strip, F32),
            pltpu.VMEM((2, 2, 2, FRAME, HALF), F32),
            pltpu.VMEM((2, 2, 2) + full_strip, F32),
            pltpu.VMEM((2,) + full_strip, F32),
            pltpu.VMEM((MODES, 2) + square, F32),
            pltpu.VMEM((2,) + square, F32),
            pltpu.VMEM((2,) + square, F32),
            pltpu.VMEM((3, 2, 64, FRAME), F32),
            pltpu.VMEM((2, 64, FRAME), F32),
            pltpu.VMEM((15, 8, FRAME), F32),
            pltpu.SemaphoreType.DMA((9,)),
            pltpu.SemaphoreType.DMA((COPIES,)),
            pltpu.SemaphoreType.DMA((COPIES,)),
        ],
        compiler_params=pltpu.CompilerParams(collective_id=1, has_side_effects=True, vmem_limit_bytes=60 << 20),
        name="gradient",
    )(positions, own, probe_modes, prop_phase, background, counts,
      jnp.asarray(lefts), jnp.asarray(rights), jnp.asarray(perm_pair))
    return near + far, probe_grad


def solution(mesh):
    in_specs = (
        P(None, None, "tile", "frame"),
        P(),
        P(),
        P(),
        P(("tile", "frame"), None),
        P(("tile", "frame"), None, None),
    )
    out_specs = (P(None, None, "tile", "frame"), P())
    return jax.shard_map(shards, mesh=mesh, in_specs=in_specs, out_specs=out_specs, check_vma=False)
```
